32 devices in a mesh: row: 8 (over z, core), col: 4 (over y, x).
Axes of the slice: x: 2, y: 2, z: 4, core: 2. Of those that a mesh axis runs over, the one named last changes fastest.
Arguments:
- patches: bfloat16 [8, 4, 2, 16, 128, 128], P('row', 'col'), as said below
- windows: bfloat16 [8, 4, 2, 16, 36864], P('row', 'col'), as said below
- candidates: int32 [8, 4, 2, 2, 128], P('row', 'col'), may hold values from -32 to 32, as said below
- live: int32 [8, 4, 2], replicated, may hold values from 1 to 16, as said below
- edges: int32 [8, 2, 2820], P('row', None, 'col'), may hold values from 0 to 255, as said below
- stiffness: float32 [8, 2820], P('row', 'col'), may hold values from 0.3 to 3
Outputs:
- matches: float32 [8, 4, 2, 3, 16], P('row', 'col')
- mesh_shift: float32 [8, 4, 2, 256], P('row', 'col')
The draws below stay inside these ranges and needn't reach their ends.
Inputs may be any that keep to these rules, and one draw needn't show every extreme that they name: `candidates`: the candidate shifts of a patch need not be distinct. live[r, c, k] counts the live slots of seam k of tile (r, c): slots 0 to live - 1; the same for all devices. Each tile's springs are the edges of its 16 x 16 vertex grid, horizontal and vertical, and one diagonal of every cell, in any order. `windows`: window k of tile (r, c) serves the seam that tile (r, c-1) (k = 0) or tile (r-1, c) (k = 1) holds as its seam k. `patches`: patch p of seam k is scored against window p of the neighbour.
All inputs are finite; a program needn't handle non-finite values.
Results may differ from the reference program's by a relative error of at most 0.0003.
Values may be sent and summed in bfloat16 or wider, within the bound.
A program may use at most 64 MiB of HBM per device.

```python
import math
import jax
import jax.numpy as jnp
from jax import lax

PATCH = 128
REACH = 32
WIN = 192
NS = 8
P_SIZE = 16
GV = 16
E = 705
ITERS = 3
TILE_ROWS = 8
TILE_COLS = 4


def window_frame(key, flat_index):
    frame_key = jax.random.fold_in(jax.random.fold_in(key, 101), flat_index)
    return jax.random.normal(frame_key, (WIN, WIN), jnp.float32)


def shift_table(key):
    table_total = TILE_ROWS * TILE_COLS * 2 * 2 * P_SIZE * NS
    values = jax.random.randint(jax.random.fold_in(key, 202), (table_total,), -REACH, REACH + 1)
    half_way = table_total // 2
    high_spot = jax.random.randint(jax.random.fold_in(key, 203), (), 0, half_way)
    low_spot = jax.random.randint(jax.random.fold_in(key, 204), (), half_way, table_total)
    values = values.at[high_spot].set(REACH).at[low_spot].set(-REACH)
    return values.reshape(TILE_ROWS, TILE_COLS, 2, 2, P_SIZE * NS).astype(jnp.int32)


def draw_windows(key, part):

    def one_frame(flat_index):
        return window_frame(key, flat_index).astype(jnp.bfloat16).reshape(WIN * WIN)
    frames = lax.map(one_frame, jnp.arange(TILE_ROWS * TILE_COLS * 2 * P_SIZE, dtype=jnp.int32))
    return frames.reshape(TILE_ROWS, TILE_COLS, 2, P_SIZE, WIN * WIN)


def draw_candidates(key, part):
    return shift_table(key)


def draw_patches(key, part):
    shifts = shift_table(key)
    truth = jax.random.randint(jax.random.fold_in(key, 303), (TILE_ROWS, TILE_COLS, 2, P_SIZE), 0, NS)

    def one_patch(flat_index):
        slot_index = flat_index % P_SIZE
        rest_index = flat_index // P_SIZE
        seam = rest_index % 2
        tile_index = rest_index // 2
        tile_row = tile_index // TILE_COLS
        tile_col = tile_index % TILE_COLS
        near_row = (tile_row + seam) % TILE_ROWS
        near_col = (tile_col + 1 - seam) % TILE_COLS
        near_index = ((near_row * TILE_COLS + near_col) * 2 + seam) * P_SIZE + slot_index
        frame_values = window_frame(key, near_index)
        chosen = truth[tile_row, tile_col, seam, slot_index]
        move_y = shifts[tile_row, tile_col, seam, 0, slot_index * NS + chosen]
        move_x = shifts[tile_row, tile_col, seam, 1, slot_index * NS + chosen]
        cropped = lax.dynamic_slice(frame_values, (REACH + move_y, REACH + move_x), (PATCH, PATCH))
        noise = jax.random.normal(jax.random.fold_in(jax.random.fold_in(key, 404), flat_index), (PATCH, PATCH), jnp.float32)
        return (0.8 * cropped + 0.6 * noise).astype(jnp.bfloat16)
    made = lax.map(one_patch, jnp.arange(TILE_ROWS * TILE_COLS * 2 * P_SIZE, dtype=jnp.int32))
    return made.reshape(TILE_ROWS, TILE_COLS, 2, P_SIZE, PATCH, PATCH)


def draw_live(key, part):
    columns = jnp.arange(TILE_COLS, dtype=jnp.int32)
    low_end = max(P_SIZE // 4, 1)
    ramp = low_end + (P_SIZE - low_end) * columns // max(TILE_COLS - 1, 1)
    lowered = jax.random.randint(jax.random.fold_in(key, 505), (TILE_ROWS, TILE_COLS, 2), 0, low_end + 1)
    counts = jnp.clip(ramp[None, :, None] - lowered, 1, P_SIZE)
    top_row = jax.random.randint(jax.random.fold_in(key, 506), (), 0, TILE_ROWS)
    top_col = jax.random.randint(jax.random.fold_in(key, 507), (), 1, TILE_COLS)
    low_row = jax.random.randint(jax.random.fold_in(key, 508), (), 0, TILE_ROWS)
    counts = counts.at[low_row, 0, :].set(1).at[top_row, top_col, :].set(P_SIZE)
    return counts.astype(jnp.int32)


def draw_edges(key, part):
    grid = jnp.arange(GV * GV, dtype=jnp.int32).reshape(GV, GV)
    cells = TILE_ROWS * TILE_COLS
    flip = jax.random.randint(jax.random.fold_in(key, 601), (cells, (GV - 1) * (GV - 1)), 0, 2)
    diag_first = jnp.where(flip == 1, grid[:-1, 1:].reshape(-1)[None, :], grid[:-1, :-1].reshape(-1)[None, :])
    diag_second = jnp.where(flip == 1, grid[1:, :-1].reshape(-1)[None, :], grid[1:, 1:].reshape(-1)[None, :])
    fixed_first = jnp.concatenate([grid[:, :-1].reshape(-1), grid[:-1, :].reshape(-1)])
    fixed_second = jnp.concatenate([grid[:, 1:].reshape(-1), grid[1:, :].reshape(-1)])
    first_ends = jnp.concatenate([jnp.broadcast_to(fixed_first[None, :], (cells, fixed_first.shape[0])), diag_first], axis=1)
    second_ends = jnp.concatenate([jnp.broadcast_to(fixed_second[None, :], (cells, fixed_second.shape[0])), diag_second], axis=1)

    def one_order(order_key):
        return jax.random.permutation(order_key, E)
    orders = jax.vmap(one_order)(jax.random.split(jax.random.fold_in(key, 602), cells))
    first_ends = jnp.take_along_axis(first_ends, orders, axis=1)
    second_ends = jnp.take_along_axis(second_ends, orders, axis=1)
    paired = jnp.stack([first_ends, second_ends], axis=1)
    paired = paired.reshape(TILE_ROWS, TILE_COLS, 2, E).transpose(0, 2, 1, 3)
    return paired.reshape(TILE_ROWS, 2, TILE_COLS * E).astype(jnp.int32)


def block_scale(rng, shape, cuts, low, high):
    gain = 1.0
    for position, blocks in cuts:
        draws = jax.random.uniform(jax.random.fold_in(jax.random.fold_in(rng, 6), position), (blocks,), jnp.float32, low / len(cuts), high / len(cuts))
        gain = gain * jnp.repeat(jnp.exp(draws), shape[position] // blocks).reshape((-1,) + (1,) * (len(shape) - 1 - position))
    return gain


def setup_inputs(seed: int = 0) -> dict:
    splits = jax.random.split(jax.random.key(seed), 7)
    return {
        "patches": draw_patches(jax.random.fold_in(splits[6], 71), 0),
        "windows": draw_windows(jax.random.fold_in(splits[6], 71), 0),
        "candidates": draw_candidates(jax.random.fold_in(splits[6], 71), 0),
        "live": draw_live(jax.random.fold_in(splits[6], 71), 0),
        "edges": draw_edges(jax.random.fold_in(splits[6], 71), 0),
        "stiffness": jnp.clip(jnp.exp(math.log(3.0) - 2.3025851 * jax.random.uniform(splits[5], (TILE_ROWS, TILE_COLS * E), jnp.float32) ** block_scale(splits[5], (TILE_ROWS, TILE_COLS * E), ((0, 8), (1, 4)), -0.2, 0.2)), 0.3, 3.0),
    }


LAMBDA_REG = 0.05
EPSILON = 1e-05
PRECISE = lax.Precision.HIGHEST

def match_block(patch_raw, frames, list_y, list_x):
    patch_size = patch_raw.shape[-1]
    cand_count = list_y.shape[-1]
    pixel_count = float(patch_size * patch_size)
    frame_pixels_all = frames.reshape(frames.shape[0], WIN, WIN)

    def crop_all(frame_pixels, shifts_y, shifts_x):

        def crop_one(move_y, move_x):
            return lax.dynamic_slice(frame_pixels, (REACH + move_y, REACH + move_x), (patch_size, patch_size))
        return jax.vmap(crop_one)(shifts_y, shifts_x)
    cropped = jax.vmap(crop_all)(frame_pixels_all, list_y, list_x)
    unit_plane = jnp.ones((patch_size, patch_size), patch_raw.dtype)
    patch_sum = jnp.einsum('byx,yx->b', patch_raw, unit_plane, preferred_element_type=jnp.float32)
    patch_square = jnp.einsum('byx,byx->b', patch_raw, patch_raw, preferred_element_type=jnp.float32)
    crop_sum = jnp.einsum('bsyx,yx->bs', cropped, unit_plane, preferred_element_type=jnp.float32)
    crop_square = jnp.einsum('bsyx,bsyx->bs', cropped, cropped, preferred_element_type=jnp.float32)
    cross_sum = jnp.einsum('byx,bsyx->bs', patch_raw, cropped, preferred_element_type=jnp.float32)
    patch_mean = patch_sum / pixel_count
    crop_mean = crop_sum / pixel_count
    patch_var = patch_square / pixel_count - patch_mean * patch_mean
    crop_var = crop_square / pixel_count - crop_mean * crop_mean
    cross_mean = cross_sum / pixel_count - patch_mean[:, None] * crop_mean
    correl = cross_mean / jnp.sqrt((patch_var[:, None] + EPSILON) * (crop_var + EPSILON))
    weight = (1.5 + correl) * (1.5 + correl)
    weight_sum = lax.optimization_barrier(jnp.sum(weight, axis=1))
    along_y = lax.optimization_barrier(jnp.sum(weight * list_y.astype(jnp.float32), axis=1)) / (REACH * weight_sum)
    along_x = lax.optimization_barrier(jnp.sum(weight * list_x.astype(jnp.float32), axis=1)) / (REACH * weight_sum)
    return jnp.stack([along_y, along_x, weight_sum / cand_count])

def reference(patches, windows, candidates, live, edges, stiffness):
    rows_all = TILE_ROWS
    cols_all = TILE_COLS
    slots = jnp.arange(P_SIZE)

    def tile_matches(flat_index):
        tile_row = flat_index // cols_all
        tile_col = flat_index % cols_all
        results = []
        for seam in range(2):
            near_row = jnp.minimum(tile_row + seam, rows_all - 1)
            near_col = jnp.minimum(tile_col + 1 - seam, cols_all - 1)
            exists = (tile_row + seam < rows_all) & (tile_col + 1 - seam < cols_all)
            live_count = jnp.where(exists, live[tile_row, tile_col, seam], 0)
            shift_grid = candidates[tile_row, tile_col, seam].reshape(2, P_SIZE, NS)
            scored = match_block(patches[tile_row, tile_col, seam], windows[near_row, near_col, seam], shift_grid[0], shift_grid[1])
            results.append(scored * (slots < live_count).astype(jnp.float32))
        return jnp.stack(results)
    matches = lax.map(tile_matches, jnp.arange(rows_all * cols_all, dtype=jnp.int32))
    matches = matches.reshape(rows_all, cols_all, 2, 3, P_SIZE)
    picker = (jnp.arange(GV)[None, :] == (slots * GV // P_SIZE)[:, None]).astype(jnp.float32)

    def spread(values):
        return jnp.einsum('rcap,pg->rcag', values, picker, precision=PRECISE)

    def sample(values):
        return jnp.einsum('rcag,pg->rcap', values, picker, precision=PRECISE)

    def from_left(values):
        return jnp.concatenate([jnp.zeros_like(values[:, :1]), values[:, :-1]], axis=1)

    def from_right(values):
        return jnp.concatenate([values[:, 1:], jnp.zeros_like(values[:, :1])], axis=1)

    def from_above(values):
        return jnp.concatenate([jnp.zeros_like(values[:1]), values[:-1]], axis=0)

    def from_below(values):
        return jnp.concatenate([values[1:], jnp.zeros_like(values[:1])], axis=0)
    conf_east = matches[:, :, 0, 2][:, :, None]
    conf_south = matches[:, :, 1, 2][:, :, None]
    shift_east = matches[:, :, 0, :2]
    shift_south = matches[:, :, 1, :2]
    conf_west = from_left(conf_east)
    shift_west = from_left(shift_east)
    conf_north = from_above(conf_south)
    shift_north = from_above(shift_south)
    endpoints = edges.reshape(rows_all, 2, cols_all, E).transpose(0, 2, 1, 3)
    spring = stiffness.reshape(rows_all, cols_all, E)

    def intra_tile(flat_field, ends, strength):
        stretch = (flat_field[:, ends[0]] - flat_field[:, ends[1]]) * strength
        return jnp.zeros_like(flat_field).at[:, ends[0]].add(stretch).at[:, ends[1]].add(-stretch)
    intra = jax.vmap(jax.vmap(intra_tile))

    def operate(vector):
        flat_field = vector.reshape(rows_all, cols_all, 2, GV * GV)
        output = (LAMBDA_REG * flat_field + intra(flat_field, endpoints, spring)).reshape(vector.shape)
        output = output.at[..., :, GV - 1].add(spread(conf_east * sample(vector[..., :, GV - 1] - from_right(vector[..., :, 0]))))
        output = output.at[..., :, 0].add(spread(conf_west * sample(vector[..., :, 0] - from_left(vector[..., :, GV - 1]))))
        output = output.at[..., GV - 1, :].add(spread(conf_south * sample(vector[..., GV - 1, :] - from_below(vector[..., 0, :]))))
        output = output.at[..., 0, :].add(spread(conf_north * sample(vector[..., 0, :] - from_above(vector[..., GV - 1, :]))))
        return output
    forcing = jnp.zeros((rows_all, cols_all, 2, GV, GV), jnp.float32)
    forcing = forcing.at[..., :, GV - 1].add(spread(conf_east * shift_east))
    forcing = forcing.at[..., :, 0].add(-spread(conf_west * shift_west))
    forcing = forcing.at[..., GV - 1, :].add(spread(conf_south * shift_south))
    forcing = forcing.at[..., 0, :].add(-spread(conf_north * shift_north))
    solution = jnp.zeros_like(forcing)
    residual = forcing
    direction = forcing
    norm_now = jnp.sum(residual * residual)
    for iteration in range(ITERS):
        applied = operate(direction)
        step_length = norm_now / jnp.sum(direction * applied)
        solution = solution + step_length * direction
        residual = residual - step_length * applied
        norm_next = jnp.sum(residual * residual)
        direction = residual + norm_next / norm_now * direction
        norm_now = norm_next
    return (matches, solution.reshape(rows_all, cols_all, 2, GV * GV))
```

```python
import functools

import jax
import jax.numpy as jnp
from jax import lax
from jax.experimental import pallas as pl
from jax.experimental.pallas import tpu as pltpu
from jax.sharding import PartitionSpec as P

REACH = 32
WIN = 192
NS = 8
P_SIZE = 16
GV = 16
CELLS = GV * GV
ITERS = 3
GAPS = (1, GV, GV + 1, GV - 1)
CHUNK = 2
PARTS = P_SIZE // CHUNK
PIECES = 3

LAMBDA_REG = 0.05
EPSILON = 1e-05
PRECISE = lax.Precision.HIGHEST
MESH = pl.DeviceIdType.MESH
HALF = P_SIZE // 2


def lane_of(seam, slot):
    west = jnp.where(slot < HALF, slot * GV, (slot - HALF) * GV + 3)
    north = jnp.where(slot < HALF, slot + 8, slot + 16)
    return jnp.where(seam == 0, west, north)


def turn(values, amount, axis=1):
    return pltpu.roll(values, amount % values.shape[axis], axis)


def montage_kernel(
    sizes, patches, windows, cands, live, edges, stiffness, matches, shift,
    held, frames, flat, plane, red, acc, cand_rows, cand_smem, live_smem, edge_rows, stiff_row,
    springs, coefs, scores, field,
    patch_send, patch_recv, cand_send, cand_recv, frame_sem, small_sem,
    col_send, col_recv, row_send, row_recv, score_send, score_recv,
):
    rows, cols = sizes
    tiles = rows * cols
    me_row = lax.axis_index("row")
    me_col = lax.axis_index("col")
    me = me_row * cols + me_col
    gives = (me_col < cols - 1, me_row < rows - 1)
    takes = (me_col > 0, me_row > 0)
    ahead = ((me_row, me_col + 1), (me_row + 1, me_col))
    pitch = windows.shape[-1] // 128 + 1
    patch_size = patches.shape[-1]
    half = patch_size // 2
    pixel_count = float(patch_size * patch_size)

    def wrap(value, count):
        return jnp.where(value >= count, value - count, value)

    def each_peer(act):
        for step in range(1, cols):
            act(me_row, wrap(me_col + step, cols))

        def one_row(step, carry):
            for col_step in range(cols):
                act(wrap(me_row + step, rows), wrap(me_col + col_step, cols))
            return carry

        lax.fori_loop(1, rows, one_row, 0)

    lanes_each = windows.shape[-1] // PIECES

    def frame_copy(seam, piece):
        span = pl.ds(piece * lanes_each, lanes_each)
        return pltpu.make_async_copy(
            windows.at[seam, :, span], frames.at[seam, :, span], frame_sem.at[seam, piece]
        )

    smalls = [
        pltpu.make_async_copy(edges, edge_rows, small_sem.at[0]),
        pltpu.make_async_copy(stiffness, stiff_row, small_sem.at[1]),
        pltpu.make_async_copy(live, live_smem, small_sem.at[2]),
    ]

    barrier = pltpu.get_barrier_semaphore()
    each_peer(
        lambda row, col: pl.semaphore_signal(
            barrier, inc=1, device_id=(row, col), device_id_type=MESH
        )
    )
    for copy in smalls:
        copy.start()
    for seam in (1, 0):
        for piece in range(PIECES):
            frame_copy(seam, piece).start()
    pl.semaphore_wait(barrier, tiles - 1)

    def cand_copy(seam):
        return pltpu.make_async_remote_copy(
            src_ref=cands.at[seam], dst_ref=cand_rows.at[seam],
            send_sem=cand_send.at[seam], recv_sem=cand_recv.at[seam],
            device_id=ahead[seam], device_id_type=MESH,
        )

    def patch_copy(seam, part):
        span = pl.ds(part * CHUNK, CHUNK)
        return pltpu.make_async_remote_copy(
            src_ref=patches.at[seam, span], dst_ref=held.at[seam, span],
            send_sem=patch_send.at[seam, part], recv_sem=patch_recv.at[seam, part],
            device_id=ahead[seam], device_id_type=MESH,
        )

    for seam in range(2):
        @pl.when(gives[seam])
        def _():
            cand_copy(seam).start()
            for part in range(PARTS):
                patch_copy(seam, part).start()

    smalls[0].wait()
    smalls[1].wait()
    first, second = edge_rows[0:1, :], edge_rows[1:2, :]
    lower = jnp.minimum(first, second)
    gap = jnp.abs(first - second)
    kind = lax.broadcasted_iota(jnp.int32, (8, 1), 0)
    wanted = jnp.where(
        kind == 0, GAPS[0], jnp.where(kind == 1, GAPS[1], jnp.where(kind == 2, GAPS[2], GAPS[3]))
    )
    wanted = jnp.where(kind < 4, wanted, -1)
    strength = jnp.where(gap == wanted, stiff_row[...], 0.0)
    vertex = lax.broadcasted_iota(jnp.int32, (CELLS, lower.shape[1]), 0)
    starts = jnp.where(vertex == lower, 1.0, 0.0)
    dense = lax.dot_general(
        strength, starts, (((1,), (1,)), ((), ())), precision=PRECISE,
        preferred_element_type=jnp.float32,
    )
    mine = pl.ds(pl.multiple_of(me * 8, 8), 8)
    springs[mine, :] = jnp.concatenate([dense[:4, :128], dense[:4, 128:]], axis=0)
    for step in range(1, cols):
        pltpu.make_async_remote_copy(
            src_ref=springs.at[mine], dst_ref=springs.at[mine],
            send_sem=col_send, recv_sem=col_recv,
            device_id=(me_row, wrap(me_col + step, cols)), device_id_type=MESH,
        ).start()

    def cols_all():
        block = springs.at[pl.ds(0, (cols - 1) * 8)]
        return pltpu.make_async_remote_copy(
            src_ref=block, dst_ref=block, send_sem=col_send, recv_sem=col_recv,
            device_id=(me_row, wrap(me_col + 1, cols)), device_id_type=MESH,
        )

    def rows_all():
        block = springs.at[pl.ds(0, (rows - 1) * cols * 8)]
        return pltpu.make_async_remote_copy(
            src_ref=block, dst_ref=block, send_sem=row_send, recv_sem=row_recv,
            device_id=(wrap(me_row + 1, rows), me_col), device_id_type=MESH,
        )

    for seam in (1, 0):
        for piece in range(PIECES):
            frame_copy(seam, piece).wait()

        @pl.when(takes[seam])
        def _():
            def spread_chunk(chunk, carry):
                start = pl.multiple_of(chunk * 128, 128)
                values = frames[seam, :, pl.ds(start, 128)].astype(jnp.float32)
                flat[pl.ds(seam * P_SIZE * pitch + chunk, P_SIZE, stride=pitch), :] = values
                return carry

            lax.fori_loop(0, pitch - 1, spread_chunk, 0, unroll=8)

    for seam in range(2):
        @pl.when(jnp.logical_not(takes[seam]))
        def _():
            cand_rows[seam] = jnp.zeros(cand_rows.shape[1:], jnp.int32)

        @pl.when(takes[seam])
        def _():
            cand_copy(seam).wait_recv()

    to_smem = pltpu.make_async_copy(cand_rows, cand_smem, small_sem.at[3])
    to_smem.start()
    acc[...] = jnp.zeros_like(acc)
    lane8 = lax.broadcasted_iota(jnp.int32, (8, 128), 1)
    lane = lax.broadcasted_iota(jnp.int32, (half, 128), 1)
    to_smem.wait()
    smalls[2].wait()

    def fold(values):
        return jnp.sum(values.reshape(half // 8, 8, 128), axis=0)

    def one_slot(seam, slot):
        plane[...] = held[seam, slot].astype(jnp.float32)
        parts = [plane[pl.ds(parity, half, stride=2), :] for parity in range(2)]
        own_sum = fold(parts[0] + parts[1])
        own_square = fold(parts[0] * parts[0] + parts[1] * parts[1])
        base = seam * P_SIZE * pitch + slot * pitch
        for cand in range(NS):
            row = REACH + cand_smem[seam, 0, slot * NS + cand]
            col = REACH + cand_smem[seam, 1, slot * NS + cand]
            crop_sum = crop_square = cross_sum = 0.0
            for parity in range(2):
                place = (row + parity) * WIN + col
                chunk = base + lax.shift_right_logical(place, 7)
                offset = lax.bitwise_and(place, 127)
                low = flat[pl.ds(chunk, half, stride=3), :]
                high = flat[pl.ds(chunk + 1, half, stride=3), :]
                crop = jnp.where(lane >= offset, low, high)
                patch = pltpu.roll(plane[pl.ds(parity, half, stride=2), :], offset, 1)
                crop_sum = crop_sum + fold(crop)
                crop_square = crop_square + fold(crop * crop)
                cross_sum = cross_sum + fold(crop * patch)
            for which, value in enumerate((crop_sum, crop_square, cross_sum)):
                red[which, cand * 8 : cand * 8 + 8, :] = value
        here = lane8 == lane_of(seam, slot)
        for which in range(5):
            if which < 3:
                value = red[which, pl.ds(0, NS, stride=8), :]
                for part in range(1, 8):
                    value = value + red[which, pl.ds(part, NS, stride=8), :]
            else:
                value = (own_sum, own_square)[which - 3]
            acc[which] = jnp.where(here, jnp.sum(value, axis=1, keepdims=True), acc[which])

    def spring_class(which):
        return jnp.concatenate(
            [springs[pl.ds(part * 4 + which, tiles, stride=8), :] for part in range(2)], axis=1
        )

    def one_part(part, carry):
        @pl.when(part == 1)
        def _():
            cols_all().wait_recv()
            band = pl.ds(pl.multiple_of(me_row * cols * 8, 8), cols * 8)

            def send_band(step, inner):
                pltpu.make_async_remote_copy(
                    src_ref=springs.at[band], dst_ref=springs.at[band],
                    send_sem=row_send, recv_sem=row_recv,
                    device_id=(wrap(me_row + step, rows), me_col), device_id_type=MESH,
                ).start()
                return inner

            lax.fori_loop(1, rows, send_band, 0)

        @pl.when(part == PARTS - 2)
        def _():
            rows_all().wait_recv()
            right, down, diag, anti = [spring_class(which) for which in range(4)]
            coefs[0] = right
            coefs[1] = turn(diag, GV)
            coefs[2] = turn(anti, -1)
            coefs[3] = turn(right, 1)
            coefs[4] = turn(diag, 1)
            coefs[5] = turn(anti, GV)
            coefs[6] = down
            coefs[7] = turn(down, GV)
            coefs[8] = (
                LAMBDA_REG + right + coefs[3] + down + coefs[7]
                + diag + turn(diag, GV + 1) + anti + turn(anti, GV - 1)
            )

        for seam in (1, 0):
            @pl.when(takes[seam])
            def _():
                patch_copy(seam, part).wait_recv()

                def slot_step(step, inner):
                    one_slot(seam, part * CHUNK + step)
                    return inner

                lax.fori_loop(0, CHUNK, slot_step, 0)
        return carry

    lax.fori_loop(0, PARTS, one_part, 0)

    index = lax.broadcasted_iota(jnp.int32, (8, 128), 1)
    member = lax.broadcasted_iota(jnp.int32, (8, 128), 0)
    pick = index % NS == member
    listed = [
        jnp.concatenate(
            [jnp.where(pick, cand_rows[seam, axis : axis + 1, :].astype(jnp.float32), 0.0)
             for seam in range(2)], axis=1,
        )
        for axis in range(2)
    ]
    listed = jnp.concatenate(listed, axis=0).astype(jnp.bfloat16)
    source = lax.broadcasted_iota(jnp.int32, (2 * P_SIZE * NS, 128), 0)
    target = lax.broadcasted_iota(jnp.int32, (2 * P_SIZE * NS, 128), 1)
    place = lane_of(
        jnp.where(source < P_SIZE * NS, 0, 1), (source % (P_SIZE * NS)) // NS
    )
    moves = jnp.dot(
        listed, jnp.where(target == place, 1.0, 0.0).astype(jnp.bfloat16),
        preferred_element_type=jnp.float32,
    )
    crop_mean, crop_square, cross_mean = [acc[n] / pixel_count for n in range(3)]
    patch_mean, patch_square = [
        jnp.sum(acc[n], axis=0, keepdims=True) / pixel_count for n in (3, 4)
    ]
    patch_var = patch_square - patch_mean * patch_mean
    crop_var = crop_square - crop_mean * crop_mean
    cross = cross_mean - patch_mean * crop_mean
    correl = cross / jnp.sqrt((patch_var + EPSILON) * (crop_var + EPSILON))
    weight = (1.5 + correl) * (1.5 + correl)
    weight_sum = jnp.sum(weight, axis=0, keepdims=True)
    along_y = jnp.sum(weight * moves[:8], axis=0, keepdims=True) / (REACH * weight_sum)
    along_x = jnp.sum(weight * moves[8:], axis=0, keepdims=True) / (REACH * weight_sum)
    spot = lax.broadcasted_iota(jnp.int32, (1, 128), 1)
    group, within = spot // GV, spot % GV
    counts = (
        jnp.where(takes[0], live_smem[jnp.maximum(me_col - 1, 0), 0, me_row], 0),
        jnp.where(takes[1], live_smem[me_col, 1, jnp.maximum(me_row - 1, 0)], 0),
    )
    western = ((within == 0) & (group < counts[0])) | ((within == 3) & (group + HALF < counts[0]))
    northern = (within >= 8) & (
        ((group == 0) & (spot - 8 < counts[1])) | ((group == 1) & (spot - 16 < counts[1]))
    )
    confidence = jnp.where(western | northern, weight_sum / NS, 0.0)
    row = confidence
    for offset, values in ((1, along_y), (2, along_x)):
        row = row + turn(jnp.where(western, values, 0.0), offset)
    for offset, values in ((32, along_y), (64, along_x)):
        row = row + turn(jnp.where(northern, values, 0.0), offset)
    scores[me] = row

    each_peer(
        lambda there_row, there_col: pltpu.make_async_remote_copy(
            src_ref=scores.at[me], dst_ref=scores.at[me],
            send_sem=score_send, recv_sem=score_recv,
            device_id=(there_row, there_col), device_id_type=MESH,
        ).start()
    )
    others = scores.at[pl.ds(0, tiles - 1)]
    scores_all = pltpu.make_async_remote_copy(
        src_ref=others, dst_ref=others, send_sem=score_send, recv_sem=score_recv,
        device_id=(me_row, wrap(me_col + 1, cols)), device_id_type=MESH,
    )
    scores_all.wait_recv()

    table = scores[...].reshape(tiles, 128)
    spot = lax.broadcasted_iota(jnp.int32, (tiles, 128), 1)
    west_lane = spot % GV == 0

    def westward(which):
        return jnp.concatenate(
            [jnp.where(west_lane, turn(table, -(which + 3 * part)), 0.0) for part in range(2)],
            axis=1,
        )

    def northward(which):
        low = turn(table, -(8 + 32 * which))
        high = turn(table, -(16 + 32 * which))
        near = jnp.where(spot < 8, low, jnp.where(spot < 16, high, 0.0))
        return jnp.concatenate([near, jnp.zeros_like(near)], axis=1)

    west, north = westward(0), northward(0)

    def eastern(values):
        return turn(turn(values, GV - 1), -1, 0)

    def southern(values):
        return turn(turn(values, -GV), -cols, 0)

    center = coefs[8] + west + north + eastern(west) + southern(north)
    forces = []
    for axis in range(2):
        pull_west, pull_north = west * westward(axis + 1), north * northward(axis + 1)
        forces.append(eastern(pull_west) + southern(pull_north) - pull_west - pull_north)

    def both(values):
        return jnp.concatenate([values, values], axis=0)

    center = both(center)
    forcing = jnp.concatenate(forces, axis=0)
    seam_west = both(turn(west, -1))
    seam_east = both(turn(west, GV))
    seam_south = both(turn(north, -GV))
    seam_north = both(north)

    def operate(vector):
        below, above = turn(vector, -GV), turn(vector, GV)
        onward = both(coefs[0]) * vector + both(coefs[1]) * above + both(coefs[2]) * below
        onward = onward + seam_west * turn(below, 1, 0)
        backward = both(coefs[3]) * vector + both(coefs[4]) * below + both(coefs[5]) * above
        backward = backward + turn(seam_east * above, -1, 0)
        straight = both(coefs[6]) * below + both(coefs[7]) * above
        straight = straight + turn(seam_south * below, -cols, 0)
        straight = straight + seam_north * turn(above, cols, 0)
        return center * vector - straight - turn(onward, 1) - turn(backward, -1)

    def total(values):
        values = values.reshape(2 * tiles // 8, 8, CELLS)
        values = jnp.sum(values, axis=0)
        values = values[:, :128] + values[:, 128:]
        return jnp.sum(jnp.sum(values, axis=0, keepdims=True), axis=1, keepdims=True)

    residual = forcing
    direction = forcing
    answer = jnp.zeros_like(forcing)
    norm_now = total(residual * residual)
    for iteration in range(ITERS):
        image = operate(direction)
        step_length = norm_now / total(direction * image)
        answer = answer + step_length * direction
        if iteration + 1 < ITERS:
            residual = residual - step_length * image
            norm_next = total(residual * residual)
            direction = residual + (norm_next / norm_now) * direction
            norm_now = norm_next
    field[...] = answer
    shift[...] = jnp.concatenate(
        [field[pl.ds(me, 1), :], field[pl.ds(tiles + me, 1), :]], axis=0
    )

    source = lax.broadcasted_iota(jnp.int32, (128, 128), 0)
    target = lax.broadcasted_iota(jnp.int32, (128, 128), 1)
    slot, quantity = target % P_SIZE, target // P_SIZE
    quantity = jnp.where(quantity == 2, 0, quantity + 1)
    for seam in range(2):
        near = ((me_row, jnp.minimum(me_col + 1, cols - 1)),
                (jnp.minimum(me_row + 1, rows - 1), me_col))[seam]
        values = jnp.where(gives[seam], scores[near[0] * cols + near[1]], 0.0)
        spread = (1, 32)[seam]
        chosen = source == lane_of(seam, slot) + quantity * spread
        chosen = jnp.where(chosen & (target < 3 * P_SIZE), 1.0, 0.0)
        packed = jnp.dot(
            jnp.concatenate([values, jnp.zeros((7, 128), jnp.float32)], axis=0), chosen,
            precision=PRECISE, preferred_element_type=jnp.float32,
        )
        for which in range(3):
            matches[which, seam : seam + 1, :] = packed[
                0:1, which * P_SIZE : (which + 1) * P_SIZE
            ]

    scores_all.wait_send()
    cols_all().wait_send()
    rows_all().wait_send()
    for seam in range(2):
        @pl.when(gives[seam])
        def _():
            cand_copy(seam).wait_send()
            for part in range(PARTS):
                patch_copy(seam, part).wait_send()


def montage_call(patches, windows, cands, live, edges, stiffness):
    rows = lax.axis_size("row")
    cols = lax.axis_size("col")
    tiles = rows * cols
    patch_size = patches.shape[-1]
    pitch = windows.shape[-1] // 128 + 1
    anywhere = pl.BlockSpec(memory_space=pl.ANY)
    vmem = pl.BlockSpec(memory_space=pltpu.VMEM)
    dma = pltpu.SemaphoreType.DMA
    f32 = jnp.float32
    return pl.pallas_call(
        functools.partial(montage_kernel, (rows, cols)),
        out_shape=(
            jax.ShapeDtypeStruct((3, 2, P_SIZE), f32),
            jax.ShapeDtypeStruct((2, CELLS), f32),
        ),
        in_specs=[anywhere] * 6,
        out_specs=(vmem, vmem),
        scratch_shapes=[
            pltpu.VMEM(patches.shape, patches.dtype),
            pltpu.VMEM(windows.shape, windows.dtype),
            pltpu.VMEM((2 * P_SIZE * pitch, 128), f32),
            pltpu.VMEM((patch_size, patch_size), f32),
            pltpu.VMEM((3, NS * 8, 128), f32),
            pltpu.VMEM((5, 8, 128), f32),
            pltpu.VMEM(cands.shape, cands.dtype),
            pltpu.SMEM(cands.shape, cands.dtype),
            pltpu.SMEM(live.shape, live.dtype),
            pltpu.VMEM(edges.shape, edges.dtype),
            pltpu.VMEM(stiffness.shape, stiffness.dtype),
            pltpu.VMEM((tiles * 8, 128), f32),
            pltpu.VMEM((9, tiles, CELLS), f32),
            pltpu.VMEM((tiles, 1, 128), f32),
            pltpu.VMEM((2 * tiles, CELLS), f32),
            dma((2, PARTS)),
            dma((2, PARTS)),
            dma((2,)),
            dma((2,)),
            dma((2, PIECES)),
            dma((4,)),
            dma, dma, dma, dma, dma, dma,
        ],
        compiler_params=pltpu.CompilerParams(
            collective_id=0, has_side_effects=True, vmem_limit_bytes=56 * 1024 * 1024
        ),
        name="montage",
    )(patches, windows, cands, live, edges, stiffness)


def body(patches, windows, candidates, live, edges, stiffness):
    matches, mesh_shift = montage_call(
        patches[0, 0], windows[0, 0], candidates[0, 0], live.transpose(1, 2, 0), edges[0],
        stiffness,
    )
    return (matches.transpose(1, 0, 2)[None, None], mesh_shift[None, None])


def solution(mesh):
    return jax.shard_map(
        body,
        mesh=mesh,
        in_specs=(
            P("row", "col", None, None, None, None),
            P("row", "col", None, None, None),
            P("row", "col", None, None, None),
            P(),
            P("row", None, "col"),
            P("row", "col"),
        ),
        out_specs=(P("row", "col", None, None, None), P("row", "col", None, None)),
        check_vma=False,
    )
```

```python
import functools

import jax
import jax.numpy as jnp
from jax import lax
from jax.experimental import pallas as pl
from jax.experimental.pallas import tpu as pltpu
from jax.sharding import PartitionSpec as P

REACH = 32
WIN = 192
NS = 8
P_SIZE = 16
GV = 16
CELLS = GV * GV
ITERS = 3
GAPS = (1, GV, GV + 1, GV - 1)
CHUNK = 2
PARTS = P_SIZE // CHUNK
PIECES = 3
AHEAD = 2
VMEM_GRANT = 56 * 1024 * 1024

LAMBDA_REG = 0.05
EPSILON = 1e-05
PRECISE = lax.Precision.HIGHEST
MESH = pl.DeviceIdType.MESH
HALF = P_SIZE // 2


def lane_of(seam, slot):
    west = jnp.where(slot < HALF, slot * GV, (slot - HALF) * GV + 3)
    north = jnp.where(slot < HALF, slot + 8, slot + 16)
    return jnp.where(seam == 0, west, north)


def turn(values, amount, axis=1):
    return pltpu.roll(values, amount % values.shape[axis], axis)


def montage_kernel(
    sizes, patches, windows, cands, live, edges, stiffness, scores, coefs_out,
    held, frames, flat, plane, red, acc, cand_rows, cand_smem, live_smem, edge_rows, stiff_row,
    springs, coefs, own_row,
    patch_send, patch_recv, cand_send, cand_recv, frame_sem, small_sem,
    col_send, col_recv, row_send, row_recv, score_send, score_recv,
):
    rows, cols = sizes
    tiles = rows * cols
    me_row = lax.axis_index("row")
    me_col = lax.axis_index("col")
    me = me_row * cols + me_col
    gives = (me_col < cols - 1, me_row < rows - 1)
    takes = (me_col > 0, me_row > 0)
    ahead = ((me_row, me_col + 1), (me_row + 1, me_col))
    pitch = windows.shape[-1] // 128 + 1
    patch_size = patches.shape[-1]
    half = patch_size // 2
    pixel_count = float(patch_size * patch_size)

    def wrap(value, count):
        return jnp.where(value >= count, value - count, value)

    def each_peer(act):
        for step in range(1, cols):
            act(me_row, wrap(me_col + step, cols))

        def one_row(step, carry):
            for col_step in range(cols):
                act(wrap(me_row + step, rows), wrap(me_col + col_step, cols))
            return carry

        lax.fori_loop(1, rows, one_row, 0)

    lanes_each = windows.shape[-1] // PIECES

    def frame_copy(seam, piece):
        span = pl.ds(piece * lanes_each, lanes_each)
        return pltpu.make_async_copy(
            windows.at[seam, :, span], frames.at[seam, :, span], frame_sem.at[seam, piece]
        )

    smalls = [
        pltpu.make_async_copy(edges, edge_rows, small_sem.at[0]),
        pltpu.make_async_copy(stiffness, stiff_row, small_sem.at[1]),
        pltpu.make_async_copy(live, live_smem, small_sem.at[2]),
    ]

    barrier = pltpu.get_barrier_semaphore()
    each_peer(
        lambda row, col: pl.semaphore_signal(
            barrier, inc=1, device_id=(row, col), device_id_type=MESH
        )
    )
    for copy in smalls:
        copy.start()
    for seam in (1, 0):
        for piece in range(PIECES):
            frame_copy(seam, piece).start()
    pl.semaphore_wait(barrier, tiles - 1)

    def cand_copy(seam):
        return pltpu.make_async_remote_copy(
            src_ref=cands.at[seam], dst_ref=cand_rows.at[seam],
            send_sem=cand_send.at[seam], recv_sem=cand_recv.at[seam],
            device_id=ahead[seam], device_id_type=MESH,
        )

    def patch_copy(seam, part):
        span = pl.ds(part * CHUNK, CHUNK)
        return pltpu.make_async_remote_copy(
            src_ref=patches.at[seam, span], dst_ref=held.at[seam, span],
            send_sem=patch_send.at[seam, part], recv_sem=patch_recv.at[seam, part],
            device_id=ahead[seam], device_id_type=MESH,
        )

    for seam in range(2):
        @pl.when(gives[seam])
        def _():
            cand_copy(seam).start()
            for part in range(AHEAD):
                patch_copy(seam, part).start()

    smalls[0].wait()
    smalls[1].wait()
    first, second = edge_rows[0:1, :], edge_rows[1:2, :]
    lower = jnp.minimum(first, second)
    gap = jnp.abs(first - second)
    kind = lax.broadcasted_iota(jnp.int32, (8, 1), 0)
    wanted = jnp.where(
        kind == 0, GAPS[0], jnp.where(kind == 1, GAPS[1], jnp.where(kind == 2, GAPS[2], GAPS[3]))
    )
    wanted = jnp.where(kind < 4, wanted, -1)
    strength = jnp.where(gap == wanted, stiff_row[...], 0.0)
    vertex = lax.broadcasted_iota(jnp.int32, (CELLS, lower.shape[1]), 0)
    starts = jnp.where(vertex == lower, 1.0, 0.0)
    dense = lax.dot_general(
        strength, starts, (((1,), (1,)), ((), ())), precision=PRECISE,
        preferred_element_type=jnp.float32,
    )
    mine = pl.ds(pl.multiple_of(me * 8, 8), 8)
    springs[mine, :] = jnp.concatenate([dense[:4, :128], dense[:4, 128:]], axis=0)
    for step in range(1, cols):
        pltpu.make_async_remote_copy(
            src_ref=springs.at[mine], dst_ref=springs.at[mine],
            send_sem=col_send, recv_sem=col_recv,
            device_id=(me_row, wrap(me_col + step, cols)), device_id_type=MESH,
        ).start()

    def cols_all():
        block = springs.at[pl.ds(0, (cols - 1) * 8)]
        return pltpu.make_async_remote_copy(
            src_ref=block, dst_ref=block, send_sem=col_send, recv_sem=col_recv,
            device_id=(me_row, wrap(me_col + 1, cols)), device_id_type=MESH,
        )

    def rows_all():
        block = springs.at[pl.ds(0, (rows - 1) * cols * 8)]
        return pltpu.make_async_remote_copy(
            src_ref=block, dst_ref=block, send_sem=row_send, recv_sem=row_recv,
            device_id=(wrap(me_row + 1, rows), me_col), device_id_type=MESH,
        )

    for seam in (1, 0):
        for piece in range(PIECES):
            frame_copy(seam, piece).wait()

        @pl.when(takes[seam])
        def _():
            def spread_chunk(chunk, carry):
                start = pl.multiple_of(chunk * 128, 128)
                values = frames[seam, :, pl.ds(start, 128)].astype(jnp.float32)
                flat[pl.ds(seam * P_SIZE * pitch + chunk, P_SIZE, stride=pitch), :] = values
                return carry

            lax.fori_loop(0, pitch - 1, spread_chunk, 0, unroll=8)

    for seam in range(2):
        @pl.when(jnp.logical_not(takes[seam]))
        def _():
            cand_rows[seam] = jnp.zeros(cand_rows.shape[1:], jnp.int32)

        @pl.when(takes[seam])
        def _():
            cand_copy(seam).wait_recv()

    to_smem = pltpu.make_async_copy(cand_rows, cand_smem, small_sem.at[3])
    to_smem.start()
    acc[...] = jnp.zeros_like(acc)
    lane8 = lax.broadcasted_iota(jnp.int32, (8, 128), 1)
    lane = lax.broadcasted_iota(jnp.int32, (half, 128), 1)
    to_smem.wait()
    smalls[2].wait()

    def fold(values):
        return jnp.sum(values.reshape(half // 8, 8, 128), axis=0)

    def one_slot(seam, slot):
        plane[...] = held[seam, slot].astype(jnp.float32)
        parts = [plane[pl.ds(parity, half, stride=2), :] for parity in range(2)]
        own_sum = fold(parts[0] + parts[1])
        own_square = fold(parts[0] * parts[0] + parts[1] * parts[1])
        base = seam * P_SIZE * pitch + slot * pitch
        for cand in range(NS):
            row = REACH + cand_smem[seam, 0, slot * NS + cand]
            col = REACH + cand_smem[seam, 1, slot * NS + cand]
            crop_sum = crop_square = cross_sum = 0.0
            for parity in range(2):
                place = (row + parity) * WIN + col
                chunk = base + lax.shift_right_logical(place, 7)
                offset = lax.bitwise_and(place, 127)
                low = flat[pl.ds(chunk, half, stride=3), :]
                high = flat[pl.ds(chunk + 1, half, stride=3), :]
                crop = jnp.where(lane >= offset, low, high)
                patch = pltpu.roll(plane[pl.ds(parity, half, stride=2), :], offset, 1)
                crop_sum = crop_sum + fold(crop)
                crop_square = crop_square + fold(crop * crop)
                cross_sum = cross_sum + fold(crop * patch)
            for which, value in enumerate((crop_sum, crop_square, cross_sum)):
                red[which, cand * 8 : cand * 8 + 8, :] = value
        here = lane8 == lane_of(seam, slot)
        for which in range(5):
            if which < 3:
                value = red[which, pl.ds(0, NS, stride=8), :]
                for part in range(1, 8):
                    value = value + red[which, pl.ds(part, NS, stride=8), :]
            else:
                value = (own_sum, own_square)[which - 3]
            acc[which] = jnp.where(here, jnp.sum(value, axis=1, keepdims=True), acc[which])

    coefs_copy = pltpu.make_async_copy(coefs, coefs_out, small_sem.at[4])

    def spring_class(which):
        return jnp.concatenate(
            [springs[pl.ds(part * 4 + which, tiles, stride=8), :] for part in range(2)], axis=1
        )

    def one_part(part, carry):
        for seam in range(2):
            @pl.when(gives[seam])
            def _():
                patch_copy(seam, part).wait_send()

            @pl.when(gives[seam] & (part + AHEAD < PARTS))
            def _():
                patch_copy(seam, part + AHEAD).start()

        @pl.when(part == 1)
        def _():
            cols_all().wait_recv()
            band = pl.ds(pl.multiple_of(me_row * cols * 8, 8), cols * 8)

            def send_band(step, inner):
                pltpu.make_async_remote_copy(
                    src_ref=springs.at[band], dst_ref=springs.at[band],
                    send_sem=row_send, recv_sem=row_recv,
                    device_id=(wrap(me_row + step, rows), me_col), device_id_type=MESH,
                ).start()
                return inner

            lax.fori_loop(1, rows, send_band, 0)

        @pl.when(part == PARTS - 2)
        def _():
            rows_all().wait_recv()
            right, down, diag, anti = [spring_class(which) for which in range(4)]
            coefs[0] = right
            coefs[1] = turn(diag, GV)
            coefs[2] = turn(anti, -1)
            coefs[3] = turn(right, 1)
            coefs[4] = turn(diag, 1)
            coefs[5] = turn(anti, GV)
            coefs[6] = down
            coefs[7] = turn(down, GV)
            coefs[8] = (
                LAMBDA_REG + right + coefs[3] + down + coefs[7]
                + diag + turn(diag, GV + 1) + anti + turn(anti, GV - 1)
            )
            coefs_copy.start()

        for seam in (1, 0):
            @pl.when(takes[seam])
            def _():
                patch_copy(seam, part).wait_recv()

                def slot_step(step, inner):
                    one_slot(seam, part * CHUNK + step)
                    return inner

                lax.fori_loop(0, CHUNK, slot_step, 0)
        return carry

    lax.fori_loop(0, PARTS, one_part, 0)

    index = lax.broadcasted_iota(jnp.int32, (8, 128), 1)
    member = lax.broadcasted_iota(jnp.int32, (8, 128), 0)
    pick = index % NS == member
    listed = [
        jnp.concatenate(
            [jnp.where(pick, cand_rows[seam, axis : axis + 1, :].astype(jnp.float32), 0.0)
             for seam in range(2)], axis=1,
        )
        for axis in range(2)
    ]
    listed = jnp.concatenate(listed, axis=0).astype(jnp.bfloat16)
    source = lax.broadcasted_iota(jnp.int32, (2 * P_SIZE * NS, 128), 0)
    target = lax.broadcasted_iota(jnp.int32, (2 * P_SIZE * NS, 128), 1)
    place = lane_of(
        jnp.where(source < P_SIZE * NS, 0, 1), (source % (P_SIZE * NS)) // NS
    )
    moves = jnp.dot(
        listed, jnp.where(target == place, 1.0, 0.0).astype(jnp.bfloat16),
        preferred_element_type=jnp.float32,
    )
    crop_mean, crop_square, cross_mean = [acc[n] / pixel_count for n in range(3)]
    patch_mean, patch_square = [
        jnp.sum(acc[n], axis=0, keepdims=True) / pixel_count for n in (3, 4)
    ]
    patch_var = patch_square - patch_mean * patch_mean
    crop_var = crop_square - crop_mean * crop_mean
    cross = cross_mean - patch_mean * crop_mean
    correl = cross / jnp.sqrt((patch_var + EPSILON) * (crop_var + EPSILON))
    weight = (1.5 + correl) * (1.5 + correl)
    weight_sum = jnp.sum(weight, axis=0, keepdims=True)
    along_y = jnp.sum(weight * moves[:8], axis=0, keepdims=True) / (REACH * weight_sum)
    along_x = jnp.sum(weight * moves[8:], axis=0, keepdims=True) / (REACH * weight_sum)
    spot = lax.broadcasted_iota(jnp.int32, (1, 128), 1)
    group, within = spot // GV, spot % GV
    counts = (
        jnp.where(takes[0], live_smem[jnp.maximum(me_col - 1, 0), 0, me_row], 0),
        jnp.where(takes[1], live_smem[me_col, 1, jnp.maximum(me_row - 1, 0)], 0),
    )
    western = ((within == 0) & (group < counts[0])) | ((within == 3) & (group + HALF < counts[0]))
    northern = (within >= 8) & (
        ((group == 0) & (spot - 8 < counts[1])) | ((group == 1) & (spot - 16 < counts[1]))
    )
    confidence = jnp.where(western | northern, weight_sum / NS, 0.0)
    row = confidence
    for offset, values in ((1, along_y), (2, along_x)):
        row = row + turn(jnp.where(western, values, 0.0), offset)
    for offset, values in ((32, along_y), (64, along_x)):
        row = row + turn(jnp.where(northern, values, 0.0), offset)
    own_row[...] = row
    own_copy = pltpu.make_async_copy(own_row, scores.at[me], small_sem.at[5])
    own_copy.start()

    each_peer(
        lambda there_row, there_col: pltpu.make_async_remote_copy(
            src_ref=own_row, dst_ref=scores.at[me],
            send_sem=score_send, recv_sem=score_recv,
            device_id=(there_row, there_col), device_id_type=MESH,
        ).start()
    )
    others = scores.at[pl.ds(0, tiles - 1)]
    scores_all = pltpu.make_async_remote_copy(
        src_ref=others, dst_ref=others, send_sem=score_send, recv_sem=score_recv,
        device_id=(me_row, wrap(me_col + 1, cols)), device_id_type=MESH,
    )
    scores_all.wait_recv()

    own_copy.wait()
    coefs_copy.wait()
    scores_all.wait_send()
    cols_all().wait_send()
    rows_all().wait_send()
    for seam in range(2):
        @pl.when(gives[seam])
        def _():
            cand_copy(seam).wait_send()


def solve_kernel(sizes, scores_in, coefs_in, matches, shift, scores, coefs, field, sem):
    rows, cols = sizes
    tiles = rows * cols
    me_row = lax.axis_index("row")
    me_col = lax.axis_index("col")
    me = me_row * cols + me_col
    gives = (me_col < cols - 1, me_row < rows - 1)
    fetches = [
        pltpu.make_async_copy(scores_in, scores, sem.at[0]),
        pltpu.make_async_copy(coefs_in, coefs, sem.at[1]),
    ]
    for copy in fetches:
        copy.start()
    for copy in fetches:
        copy.wait()

    table = scores[...]
    spot = lax.broadcasted_iota(jnp.int32, (tiles, 128), 1)
    west_lane = spot % GV == 0

    def westward(which):
        return jnp.concatenate(
            [jnp.where(west_lane, turn(table, -(which + 3 * part)), 0.0) for part in range(2)],
            axis=1,
        )

    def northward(which):
        low = turn(table, -(8 + 32 * which))
        high = turn(table, -(16 + 32 * which))
        near = jnp.where(spot < 8, low, jnp.where(spot < 16, high, 0.0))
        return jnp.concatenate([near, jnp.zeros_like(near)], axis=1)

    west, north = westward(0), northward(0)

    def eastern(values):
        return turn(turn(values, GV - 1), -1, 0)

    def southern(values):
        return turn(turn(values, -GV), -cols, 0)

    center = coefs[8] + west + north + eastern(west) + southern(north)
    forces = []
    for axis in range(2):
        pull_west, pull_north = west * westward(axis + 1), north * northward(axis + 1)
        forces.append(eastern(pull_west) + southern(pull_north) - pull_west - pull_north)

    def both(values):
        return jnp.concatenate([values, values], axis=0)

    center = both(center)
    forcing = jnp.concatenate(forces, axis=0)
    seam_west = both(turn(west, -1))
    seam_east = both(turn(west, GV))
    seam_south = both(turn(north, -GV))
    seam_north = both(north)

    def operate(vector):
        below, above = turn(vector, -GV), turn(vector, GV)
        onward = both(coefs[0]) * vector + both(coefs[1]) * above + both(coefs[2]) * below
        onward = onward + seam_west * turn(below, 1, 0)
        backward = both(coefs[3]) * vector + both(coefs[4]) * below + both(coefs[5]) * above
        backward = backward + turn(seam_east * above, -1, 0)
        straight = both(coefs[6]) * below + both(coefs[7]) * above
        straight = straight + turn(seam_south * below, -cols, 0)
        straight = straight + seam_north * turn(above, cols, 0)
        return center * vector - straight - turn(onward, 1) - turn(backward, -1)

    def total(values):
        values = values.reshape(2 * tiles // 8, 8, CELLS)
        values = jnp.sum(values, axis=0)
        values = values[:, :128] + values[:, 128:]
        return jnp.sum(jnp.sum(values, axis=0, keepdims=True), axis=1, keepdims=True)

    residual = forcing
    direction = forcing
    answer = jnp.zeros_like(forcing)
    norm_now = total(residual * residual)
    for iteration in range(ITERS):
        image = operate(direction)
        step_length = norm_now / total(direction * image)
        answer = answer + step_length * direction
        if iteration + 1 < ITERS:
            residual = residual - step_length * image
            norm_next = total(residual * residual)
            direction = residual + (norm_next / norm_now) * direction
            norm_now = norm_next
    field[...] = answer
    shift[...] = jnp.concatenate(
        [field[pl.ds(me, 1), :], field[pl.ds(tiles + me, 1), :]], axis=0
    )

    source = lax.broadcasted_iota(jnp.int32, (128, 128), 0)
    target = lax.broadcasted_iota(jnp.int32, (128, 128), 1)
    slot, quantity = target % P_SIZE, target // P_SIZE
    quantity = jnp.where(quantity == 2, 0, quantity + 1)
    for seam in range(2):
        near = ((me_row, jnp.minimum(me_col + 1, cols - 1)),
                (jnp.minimum(me_row + 1, rows - 1), me_col))[seam]
        values = jnp.where(gives[seam], scores[pl.ds(near[0] * cols + near[1], 1), :], 0.0)
        spread = (1, 32)[seam]
        chosen = source == lane_of(seam, slot) + quantity * spread
        chosen = jnp.where(chosen & (target < 3 * P_SIZE), 1.0, 0.0)
        packed = jnp.dot(
            jnp.concatenate([values, jnp.zeros((7, 128), jnp.float32)], axis=0), chosen,
            precision=PRECISE, preferred_element_type=jnp.float32,
        )
        for which in range(3):
            matches[which, seam : seam + 1, :] = packed[
                0:1, which * P_SIZE : (which + 1) * P_SIZE
            ]


def montage_call(patches, windows, cands, live, edges, stiffness):
    rows = lax.axis_size("row")
    cols = lax.axis_size("col")
    tiles = rows * cols
    patch_size = patches.shape[-1]
    pitch = windows.shape[-1] // 128 + 1
    anywhere = pl.BlockSpec(memory_space=pl.ANY)
    dma = pltpu.SemaphoreType.DMA
    f32 = jnp.float32
    return pl.pallas_call(
        functools.partial(montage_kernel, (rows, cols)),
        out_shape=(
            jax.ShapeDtypeStruct((tiles, 1, 128), f32),
            jax.ShapeDtypeStruct((9, tiles, CELLS), f32),
        ),
        in_specs=[anywhere] * 6,
        out_specs=(anywhere, anywhere),
        scratch_shapes=[
            pltpu.VMEM(patches.shape, patches.dtype),
            pltpu.VMEM(windows.shape, windows.dtype),
            pltpu.VMEM((2 * P_SIZE * pitch, 128), f32),
            pltpu.VMEM((patch_size, patch_size), f32),
            pltpu.VMEM((3, NS * 8, 128), f32),
            pltpu.VMEM((5, 8, 128), f32),
            pltpu.VMEM(cands.shape, cands.dtype),
            pltpu.SMEM(cands.shape, cands.dtype),
            pltpu.SMEM(live.shape, live.dtype),
            pltpu.VMEM(edges.shape, edges.dtype),
            pltpu.VMEM(stiffness.shape, stiffness.dtype),
            pltpu.VMEM((tiles * 8, 128), f32),
            pltpu.VMEM((9, tiles, CELLS), f32),
            pltpu.VMEM((1, 128), f32),
            dma((2, PARTS)),
            dma((2, PARTS)),
            dma((2,)),
            dma((2,)),
            dma((2, PIECES)),
            dma((6,)),
            dma, dma, dma, dma, dma, dma,
        ],
        compiler_params=pltpu.CompilerParams(
            collective_id=0, has_side_effects=True, vmem_limit_bytes=VMEM_GRANT
        ),
        name="montage",
    )(patches, windows, cands, live, edges, stiffness)


def solve_call(scores, coefs):
    rows = lax.axis_size("row")
    cols = lax.axis_size("col")
    tiles = rows * cols
    anywhere = pl.BlockSpec(memory_space=pl.ANY)
    vmem = pl.BlockSpec(memory_space=pltpu.VMEM)
    return pl.pallas_call(
        functools.partial(solve_kernel, (rows, cols)),
        out_shape=(
            jax.ShapeDtypeStruct((3, 2, P_SIZE), jnp.float32),
            jax.ShapeDtypeStruct((2, CELLS), jnp.float32),
        ),
        in_specs=[anywhere, anywhere],
        out_specs=(vmem, vmem),
        scratch_shapes=[
            pltpu.VMEM((tiles, 128), jnp.float32),
            pltpu.VMEM((9, tiles, CELLS), jnp.float32),
            pltpu.VMEM((2 * tiles, CELLS), jnp.float32),
            pltpu.SemaphoreType.DMA((2,)),
        ],
        compiler_params=pltpu.CompilerParams(vmem_limit_bytes=VMEM_GRANT),
        name="solve",
    )(scores.reshape(tiles, 128), coefs)


def body(patches, windows, candidates, live, edges, stiffness):
    scores, coefs = montage_call(
        patches[0, 0], windows[0, 0], candidates[0, 0], live.transpose(1, 2, 0), edges[0],
        stiffness,
    )
    matches, mesh_shift = solve_call(scores, coefs)
    return (matches.transpose(1, 0, 2)[None, None], mesh_shift[None, None])


def solution(mesh):
    return jax.shard_map(
        body,
        mesh=mesh,
        in_specs=(
            P("row", "col", None, None, None, None),
            P("row", "col", None, None, None),
            P("row", "col", None, None, None),
            P(),
            P("row", None, "col"),
            P("row", "col"),
        ),
        out_specs=(P("row", "col", None, None, None), P("row", "col", None, None)),
        check_vma=False,
    )
```

```python
import functools

import jax
import jax.numpy as jnp
from jax import lax
from jax.experimental import pallas as pl
from jax.experimental.pallas import tpu as pltpu
from jax.sharding import PartitionSpec as P

REACH = 32
WIN = 192
NS = 8
P_SIZE = 16
GV = 16
CELLS = GV * GV
ITERS = 3
GAPS = (1, GV, GV + 1, GV - 1)
CHUNK = 2
PARTS = P_SIZE // CHUNK
PIECES = 3
AHEAD = 4
ROWS_AT = 3
VMEM_GRANT = 56 * 1024 * 1024

LAMBDA_REG = 0.05
EPSILON = 1e-05
PRECISE = lax.Precision.HIGHEST
MESH = pl.DeviceIdType.MESH
HALF = P_SIZE // 2


def lane_of(seam, slot):
    west = jnp.where(slot < HALF, slot * GV, (slot - HALF) * GV + 3)
    north = jnp.where(slot < HALF, slot + 8, slot + 16)
    return jnp.where(seam == 0, west, north)


def turn(values, amount, axis=1):
    return pltpu.roll(values, amount % values.shape[axis], axis)


def rounds_of(count):
    return (count - 1).bit_length()


def partners(me, count, step):
    hop = 1 << step
    if count & (count - 1):
        return lax.rem(me + hop, count), lax.rem(me + count - hop, count)
    other = me + hop - 2 * hop * lax.rem(me // hop, 2)
    return other, other


def montage_kernel(
    sizes, patches, windows, cands, live, edges, stiffness, scores, coefs_out,
    held, frames, flat, plane, red, acc, cand_rows, cand_smem, live_smem, edge_rows, stiff_row,
    springs, coefs, own_row, moves,
    patch_send, patch_recv, cand_send, cand_recv, frame_sem, small_sem,
    col_send, col_recv, row_send, row_recv, score_send, score_recv,
    round_sem,
):
    rows, cols = sizes
    tiles = rows * cols
    me_row = lax.axis_index("row")
    me_col = lax.axis_index("col")
    me = me_row * cols + me_col
    gives = (me_col < cols - 1, me_row < rows - 1)
    takes = (me_col > 0, me_row > 0)
    ahead = ((me_row, me_col + 1), (me_row + 1, me_col))
    pitch = windows.shape[-1] // 128 + 1
    patch_size = patches.shape[-1]
    half = patch_size // 2
    pixel_count = float(patch_size * patch_size)

    def wrap(value, count):
        return jnp.where(value >= count, value - count, value)

    def each_peer(act):
        for step in range(1, cols):
            act(me_row, wrap(me_col + step, cols))

        def one_row(step, carry):
            for col_step in range(cols):
                act(wrap(me_row + step, rows), wrap(me_col + col_step, cols))
            return carry

        lax.fori_loop(1, rows, one_row, 0)

    lanes_each = windows.shape[-1] // PIECES

    def frame_copy(seam, piece):
        span = pl.ds(piece * lanes_each, lanes_each)
        return pltpu.make_async_copy(
            windows.at[seam, :, span], frames.at[seam, :, span], frame_sem.at[seam, piece]
        )

    smalls = [
        pltpu.make_async_copy(edges, edge_rows, small_sem.at[0]),
        pltpu.make_async_copy(stiffness, stiff_row, small_sem.at[1]),
        pltpu.make_async_copy(live, live_smem, small_sem.at[2]),
    ]

    barrier = pltpu.get_barrier_semaphore()
    near = [
        (gives[0], (me_row, me_col + 1)), (gives[1], (me_row + 1, me_col)),
        (takes[0], (me_row, me_col - 1)), (takes[1], (me_row - 1, me_col)),
    ]
    expected = jnp.int32(0)
    for exists, device in near:
        @pl.when(exists)
        def _():
            pl.semaphore_signal(barrier, inc=1, device_id=device, device_id_type=MESH)
        expected = expected + exists.astype(jnp.int32)
    stages = [("col", step) for step in range(rounds_of(cols))]
    stages += [("row", step) for step in range(rounds_of(rows))]

    def stage_partners(stage):
        axis, step = stages[stage]
        if axis == "col":
            return [(me_row, col) for col in partners(me_col, cols, step)]
        return [(row, me_col) for row in partners(me_row, rows, step)]

    for stage, (axis, step) in enumerate(stages):
        count = cols if axis == "col" else rows
        pair = stage_partners(stage)
        if count & (count - 1) == 0:
            pair = pair[:1] if step else []
        for device in pair:
            pl.semaphore_signal(barrier, inc=1, device_id=device, device_id_type=MESH)
        expected = expected + len(pair)
    for copy in smalls:
        copy.start()
    for seam in (1, 0):
        for piece in range(PIECES):
            frame_copy(seam, piece).start()
    pl.semaphore_wait(barrier, expected)

    def cand_copy(seam):
        return pltpu.make_async_remote_copy(
            src_ref=cands.at[seam], dst_ref=cand_rows.at[seam],
            send_sem=cand_send.at[seam], recv_sem=cand_recv.at[seam],
            device_id=ahead[seam], device_id_type=MESH,
        )

    def patch_copy(seam, part):
        span = pl.ds(part * CHUNK, CHUNK)
        return pltpu.make_async_remote_copy(
            src_ref=patches.at[seam, span], dst_ref=held.at[seam, span],
            send_sem=patch_send.at[seam, part], recv_sem=patch_recv.at[seam, part],
            device_id=ahead[seam], device_id_type=MESH,
        )

    for part in range(AHEAD):
        for seam in range(2):
            @pl.when(gives[seam])
            def _():
                patch_copy(seam, part).start()
                if part == 0:
                    cand_copy(seam).start()

    def say(stage):
        pl.semaphore_signal(
            round_sem.at[stage], inc=1, device_id=stage_partners(stage)[0], device_id_type=MESH
        )

    def hear(stage):
        pl.semaphore_wait(round_sem.at[stage], 1)
        if stage + 1 < len(stages):
            say(stage + 1)

    col_stages = rounds_of(cols)
    say(0)

    smalls[0].wait()
    smalls[1].wait()
    first, second = edge_rows[0:1, :], edge_rows[1:2, :]
    lower = jnp.minimum(first, second)
    gap = jnp.abs(first - second)
    kind = lax.broadcasted_iota(jnp.int32, (8, 1), 0)
    wanted = jnp.where(
        kind == 0, GAPS[0], jnp.where(kind == 1, GAPS[1], jnp.where(kind == 2, GAPS[2], GAPS[3]))
    )
    wanted = jnp.where(kind < 4, wanted, -1)
    strength = jnp.where(gap == wanted, stiff_row[...], 0.0)
    vertex = lax.broadcasted_iota(jnp.int32, (CELLS, lower.shape[1]), 0)
    starts = jnp.where(vertex == lower, 1.0, 0.0)
    dense = lax.dot_general(
        strength, starts, (((1,), (1,)), ((), ())), precision=PRECISE,
        preferred_element_type=jnp.float32,
    )
    mine = pl.ds(pl.multiple_of(me * 8, 8), 8)
    springs[mine, :] = jnp.concatenate([dense[:4, :128], dense[:4, 128:]], axis=0)
    hear(0)

    def send_springs():
        for step in range(1, cols):
            pltpu.make_async_remote_copy(
                src_ref=springs.at[mine], dst_ref=springs.at[mine],
                send_sem=col_send, recv_sem=col_recv,
                device_id=(me_row, wrap(me_col + step, cols)), device_id_type=MESH,
            ).start()

    def cols_all():
        block = springs.at[pl.ds(0, (cols - 1) * 8)]
        return pltpu.make_async_remote_copy(
            src_ref=block, dst_ref=block, send_sem=col_send, recv_sem=col_recv,
            device_id=(me_row, wrap(me_col + 1, cols)), device_id_type=MESH,
        )

    def rows_all():
        block = springs.at[pl.ds(0, (rows - 1) * cols * 8)]
        return pltpu.make_async_remote_copy(
            src_ref=block, dst_ref=block, send_sem=row_send, recv_sem=row_recv,
            device_id=(wrap(me_row + 1, rows), me_col), device_id_type=MESH,
        )

    for seam in (1, 0):
        for piece in range(PIECES):
            frame_copy(seam, piece).wait()

        @pl.when(takes[seam])
        def _():
            def spread_chunk(chunk, carry):
                start = pl.multiple_of(chunk * 128, 128)
                values = frames[seam, :, pl.ds(start, 128)].astype(jnp.float32)
                flat[pl.ds(seam * P_SIZE * pitch + chunk, P_SIZE, stride=pitch), :] = values
                return carry

            lax.fori_loop(0, pitch - 1, spread_chunk, 0, unroll=8)

        if seam == 1:
            for stage in range(1, col_stages):
                hear(stage)
            send_springs()

    for seam in range(2):
        @pl.when(jnp.logical_not(takes[seam]))
        def _():
            cand_rows[seam] = jnp.zeros(cand_rows.shape[1:], jnp.int32)

        @pl.when(takes[seam])
        def _():
            cand_copy(seam).wait_recv()

    to_smem = pltpu.make_async_copy(cand_rows, cand_smem, small_sem.at[3])
    to_smem.start()
    acc[...] = jnp.zeros_like(acc)
    index = lax.broadcasted_iota(jnp.int32, (8, 128), 1)
    member = lax.broadcasted_iota(jnp.int32, (8, 128), 0)
    pick = index % NS == member
    listed = [
        jnp.concatenate(
            [jnp.where(pick, cand_rows[seam, axis : axis + 1, :].astype(jnp.float32), 0.0)
             for seam in range(2)], axis=1,
        )
        for axis in range(2)
    ]
    listed = jnp.concatenate(listed, axis=0).astype(jnp.bfloat16)
    source = lax.broadcasted_iota(jnp.int32, (2 * P_SIZE * NS, 128), 0)
    target = lax.broadcasted_iota(jnp.int32, (2 * P_SIZE * NS, 128), 1)
    place = lane_of(
        jnp.where(source < P_SIZE * NS, 0, 1), (source % (P_SIZE * NS)) // NS
    )
    moves[...] = jnp.dot(
        listed, jnp.where(target == place, 1.0, 0.0).astype(jnp.bfloat16),
        preferred_element_type=jnp.float32,
    )
    lane8 = lax.broadcasted_iota(jnp.int32, (8, 128), 1)
    lane = lax.broadcasted_iota(jnp.int32, (half, 128), 1)
    to_smem.wait()
    smalls[2].wait()

    def fold(values):
        return jnp.sum(values.reshape(half // 8, 8, 128), axis=0)

    def one_slot(seam, slot):
        plane[...] = held[seam, slot].astype(jnp.float32)
        parts = [plane[pl.ds(parity, half, stride=2), :] for parity in range(2)]
        own_sum = fold(parts[0] + parts[1])
        own_square = fold(parts[0] * parts[0] + parts[1] * parts[1])
        base = seam * P_SIZE * pitch + slot * pitch
        for cand in range(NS):
            row = REACH + cand_smem[seam, 0, slot * NS + cand]
            col = REACH + cand_smem[seam, 1, slot * NS + cand]
            crop_sum = crop_square = cross_sum = 0.0
            for parity in range(2):
                place = (row + parity) * WIN + col
                chunk = base + lax.shift_right_logical(place, 7)
                offset = lax.bitwise_and(place, 127)
                low = flat[pl.ds(chunk, half, stride=3), :]
                high = flat[pl.ds(chunk + 1, half, stride=3), :]
                crop = jnp.where(lane >= offset, low, high)
                patch = pltpu.roll(plane[pl.ds(parity, half, stride=2), :], offset, 1)
                crop_sum = crop_sum + fold(crop)
                crop_square = crop_square + fold(crop * crop)
                cross_sum = cross_sum + fold(crop * patch)
            for which, value in enumerate((crop_sum, crop_square, cross_sum)):
                red[which, cand * 8 : cand * 8 + 8, :] = value
        here = lane8 == lane_of(seam, slot)
        for which in range(5):
            if which < 3:
                value = red[which, pl.ds(0, NS, stride=8), :]
                for part in range(1, 8):
                    value = value + red[which, pl.ds(part, NS, stride=8), :]
            else:
                value = (own_sum, own_square)[which - 3]
            acc[which] = jnp.where(here, jnp.sum(value, axis=1, keepdims=True), acc[which])

    coefs_copy = pltpu.make_async_copy(coefs, coefs_out, small_sem.at[4])

    def spring_class(which):
        return jnp.concatenate(
            [springs[pl.ds(part * 4 + which, tiles, stride=8), :] for part in range(2)], axis=1
        )

    def one_part(part, carry):
        for seam in range(2):
            @pl.when(gives[seam])
            def _():
                patch_copy(seam, part).wait_send()

            @pl.when(gives[seam] & (part + AHEAD < PARTS))
            def _():
                patch_copy(seam, part + AHEAD).start()

        for stage in range(col_stages, len(stages)):
            @pl.when(part == max(ROWS_AT - (len(stages) - 1 - stage), 0))
            def _():
                hear(stage)

        @pl.when(part == ROWS_AT)
        def _():
            cols_all().wait_recv()
            band = pl.ds(pl.multiple_of(me_row * cols * 8, 8), cols * 8)

            def send_band(step, inner):
                pltpu.make_async_remote_copy(
                    src_ref=springs.at[band], dst_ref=springs.at[band],
                    send_sem=row_send, recv_sem=row_recv,
                    device_id=(wrap(me_row + step, rows), me_col), device_id_type=MESH,
                ).start()
                return inner

            lax.fori_loop(1, rows, send_band, 0)

        @pl.when(part == PARTS - 1)
        def _():
            rows_all().wait_recv()
            right, down, diag, anti = [spring_class(which) for which in range(4)]
            coefs[0] = right
            coefs[1] = turn(diag, GV)
            coefs[2] = turn(anti, -1)
            coefs[3] = turn(right, 1)
            coefs[4] = turn(diag, 1)
            coefs[5] = turn(anti, GV)
            coefs[6] = down
            coefs[7] = turn(down, GV)
            coefs[8] = (
                LAMBDA_REG + right + coefs[3] + down + coefs[7]
                + diag + turn(diag, GV + 1) + anti + turn(anti, GV - 1)
            )
            coefs_copy.start()

        for seam in (1, 0):
            @pl.when(takes[seam])
            def _():
                patch_copy(seam, part).wait_recv()

                def slot_step(step, inner):
                    one_slot(seam, part * CHUNK + step)
                    return inner

                lax.fori_loop(0, CHUNK, slot_step, 0)
        return carry

    lax.fori_loop(0, PARTS, one_part, 0)

    crop_mean, crop_square, cross_mean = [acc[n] / pixel_count for n in range(3)]
    patch_mean, patch_square = [
        jnp.sum(acc[n], axis=0, keepdims=True) / pixel_count for n in (3, 4)
    ]
    patch_var = patch_square - patch_mean * patch_mean
    crop_var = crop_square - crop_mean * crop_mean
    cross = cross_mean - patch_mean * crop_mean
    correl = cross / jnp.sqrt((patch_var + EPSILON) * (crop_var + EPSILON))
    weight = (1.5 + correl) * (1.5 + correl)
    weight_sum = jnp.sum(weight, axis=0, keepdims=True)
    along_y = jnp.sum(weight * moves[:8, :], axis=0, keepdims=True) / (REACH * weight_sum)
    along_x = jnp.sum(weight * moves[8:, :], axis=0, keepdims=True) / (REACH * weight_sum)
    spot = lax.broadcasted_iota(jnp.int32, (1, 128), 1)
    group, within = spot // GV, spot % GV
    counts = (
        jnp.where(takes[0], live_smem[jnp.maximum(me_col - 1, 0), 0, me_row], 0),
        jnp.where(takes[1], live_smem[me_col, 1, jnp.maximum(me_row - 1, 0)], 0),
    )
    western = ((within == 0) & (group < counts[0])) | ((within == 3) & (group + HALF < counts[0]))
    northern = (within >= 8) & (
        ((group == 0) & (spot - 8 < counts[1])) | ((group == 1) & (spot - 16 < counts[1]))
    )
    confidence = jnp.where(western | northern, weight_sum / NS, 0.0)
    row = confidence
    for offset, values in ((1, along_y), (2, along_x)):
        row = row + turn(jnp.where(western, values, 0.0), offset)
    for offset, values in ((32, along_y), (64, along_x)):
        row = row + turn(jnp.where(northern, values, 0.0), offset)
    own_row[...] = row
    own_copy = pltpu.make_async_copy(own_row, scores.at[me], small_sem.at[5])
    own_copy.start()

    each_peer(
        lambda there_row, there_col: pltpu.make_async_remote_copy(
            src_ref=own_row, dst_ref=scores.at[me],
            send_sem=score_send, recv_sem=score_recv,
            device_id=(there_row, there_col), device_id_type=MESH,
        ).start()
    )
    others = scores.at[pl.ds(0, tiles - 1)]
    scores_all = pltpu.make_async_remote_copy(
        src_ref=others, dst_ref=others, send_sem=score_send, recv_sem=score_recv,
        device_id=(me_row, wrap(me_col + 1, cols)), device_id_type=MESH,
    )
    scores_all.wait_recv()

    own_copy.wait()
    coefs_copy.wait()
    scores_all.wait_send()
    cols_all().wait_send()
    rows_all().wait_send()
    for seam in range(2):
        @pl.when(gives[seam])
        def _():
            cand_copy(seam).wait_send()


def solve_kernel(sizes, scores_in, coefs_in, matches, shift, scores, coefs, field, sem):
    rows, cols = sizes
    tiles = rows * cols
    me_row = lax.axis_index("row")
    me_col = lax.axis_index("col")
    me = me_row * cols + me_col
    gives = (me_col < cols - 1, me_row < rows - 1)
    fetches = [
        pltpu.make_async_copy(scores_in, scores, sem.at[0]),
        pltpu.make_async_copy(coefs_in, coefs, sem.at[1]),
    ]
    for copy in fetches:
        copy.start()
    for copy in fetches:
        copy.wait()

    table = scores[...]
    spot = lax.broadcasted_iota(jnp.int32, (tiles, 128), 1)
    west_lane = spot % GV == 0

    def westward(which):
        return jnp.concatenate(
            [jnp.where(west_lane, turn(table, -(which + 3 * part)), 0.0) for part in range(2)],
            axis=1,
        )

    def northward(which):
        low = turn(table, -(8 + 32 * which))
        high = turn(table, -(16 + 32 * which))
        near = jnp.where(spot < 8, low, jnp.where(spot < 16, high, 0.0))
        return jnp.concatenate([near, jnp.zeros_like(near)], axis=1)

    west, north = westward(0), northward(0)

    def eastern(values):
        return turn(turn(values, GV - 1), -1, 0)

    def southern(values):
        return turn(turn(values, -GV), -cols, 0)

    center = coefs[8] + west + north + eastern(west) + southern(north)
    forces = []
    for axis in range(2):
        pull_west, pull_north = west * westward(axis + 1), north * northward(axis + 1)
        forces.append(eastern(pull_west) + southern(pull_north) - pull_west - pull_north)

    def both(values):
        return jnp.concatenate([values, values], axis=0)

    center = both(center)
    forcing = jnp.concatenate(forces, axis=0)
    seam_west = both(turn(west, -1))
    seam_east = both(turn(west, GV))
    seam_south = both(turn(north, -GV))
    seam_north = both(north)

    def operate(vector):
        below, above = turn(vector, -GV), turn(vector, GV)
        onward = both(coefs[0]) * vector + both(coefs[1]) * above + both(coefs[2]) * below
        onward = onward + seam_west * turn(below, 1, 0)
        backward = both(coefs[3]) * vector + both(coefs[4]) * below + both(coefs[5]) * above
        backward = backward + turn(seam_east * above, -1, 0)
        straight = both(coefs[6]) * below + both(coefs[7]) * above
        straight = straight + turn(seam_south * below, -cols, 0)
        straight = straight + seam_north * turn(above, cols, 0)
        return center * vector - straight - turn(onward, 1) - turn(backward, -1)

    def total(values):
        values = values.reshape(2 * tiles // 8, 8, CELLS)
        values = jnp.sum(values, axis=0)
        values = values[:, :128] + values[:, 128:]
        return jnp.sum(jnp.sum(values, axis=0, keepdims=True), axis=1, keepdims=True)

    residual = forcing
    direction = forcing
    answer = jnp.zeros_like(forcing)
    norm_now = total(residual * residual)
    for iteration in range(ITERS):
        image = operate(direction)
        step_length = norm_now / total(direction * image)
        answer = answer + step_length * direction
        if iteration + 1 < ITERS:
            residual = residual - step_length * image
            norm_next = total(residual * residual)
            direction = residual + (norm_next / norm_now) * direction
            norm_now = norm_next
    field[...] = answer
    shift[...] = jnp.concatenate(
        [field[pl.ds(me, 1), :], field[pl.ds(tiles + me, 1), :]], axis=0
    )

    source = lax.broadcasted_iota(jnp.int32, (128, 128), 0)
    target = lax.broadcasted_iota(jnp.int32, (128, 128), 1)
    slot, quantity = target % P_SIZE, target // P_SIZE
    quantity = jnp.where(quantity == 2, 0, quantity + 1)
    for seam in range(2):
        near = ((me_row, jnp.minimum(me_col + 1, cols - 1)),
                (jnp.minimum(me_row + 1, rows - 1), me_col))[seam]
        values = jnp.where(gives[seam], scores[pl.ds(near[0] * cols + near[1], 1), :], 0.0)
        spread = (1, 32)[seam]
        chosen = source == lane_of(seam, slot) + quantity * spread
        chosen = jnp.where(chosen & (target < 3 * P_SIZE), 1.0, 0.0)
        packed = jnp.dot(
            jnp.concatenate([values, jnp.zeros((7, 128), jnp.float32)], axis=0), chosen,
            precision=PRECISE, preferred_element_type=jnp.float32,
        )
        for which in range(3):
            matches[which, seam : seam + 1, :] = packed[
                0:1, which * P_SIZE : (which + 1) * P_SIZE
            ]


def montage_call(patches, windows, cands, live, edges, stiffness):
    rows = lax.axis_size("row")
    cols = lax.axis_size("col")
    tiles = rows * cols
    patch_size = patches.shape[-1]
    pitch = windows.shape[-1] // 128 + 1
    anywhere = pl.BlockSpec(memory_space=pl.ANY)
    dma = pltpu.SemaphoreType.DMA
    f32 = jnp.float32
    return pl.pallas_call(
        functools.partial(montage_kernel, (rows, cols)),
        out_shape=(
            jax.ShapeDtypeStruct((tiles, 1, 128), f32),
            jax.ShapeDtypeStruct((9, tiles, CELLS), f32),
        ),
        in_specs=[anywhere] * 6,
        out_specs=(anywhere, anywhere),
        scratch_shapes=[
            pltpu.VMEM(patches.shape, patches.dtype),
            pltpu.VMEM(windows.shape, windows.dtype),
            pltpu.VMEM((2 * P_SIZE * pitch, 128), f32),
            pltpu.VMEM((patch_size, patch_size), f32),
            pltpu.VMEM((3, NS * 8, 128), f32),
            pltpu.VMEM((5, 8, 128), f32),
            pltpu.VMEM(cands.shape, cands.dtype),
            pltpu.SMEM(cands.shape, cands.dtype),
            pltpu.SMEM(live.shape, live.dtype),
            pltpu.VMEM(edges.shape, edges.dtype),
            pltpu.VMEM(stiffness.shape, stiffness.dtype),
            pltpu.VMEM((tiles * 8, 128), f32),
            pltpu.VMEM((9, tiles, CELLS), f32),
            pltpu.VMEM((1, 128), f32),
            pltpu.VMEM((2 * NS, 128), f32),
            dma((2, PARTS)),
            dma((2, PARTS)),
            dma((2,)),
            dma((2,)),
            dma((2, PIECES)),
            dma((6,)),
            dma, dma, dma, dma, dma, dma,
            pltpu.SemaphoreType.REGULAR((rounds_of(rows) + rounds_of(cols),)),
        ],
        compiler_params=pltpu.CompilerParams(
            collective_id=0, has_side_effects=True, vmem_limit_bytes=VMEM_GRANT
        ),
        name="montage",
    )(patches, windows, cands, live, edges, stiffness)


def solve_call(scores, coefs):
    rows = lax.axis_size("row")
    cols = lax.axis_size("col")
    tiles = rows * cols
    anywhere = pl.BlockSpec(memory_space=pl.ANY)
    vmem = pl.BlockSpec(memory_space=pltpu.VMEM)
    return pl.pallas_call(
        functools.partial(solve_kernel, (rows, cols)),
        out_shape=(
            jax.ShapeDtypeStruct((3, 2, P_SIZE), jnp.float32),
            jax.ShapeDtypeStruct((2, CELLS), jnp.float32),
        ),
        in_specs=[anywhere, anywhere],
        out_specs=(vmem, vmem),
        scratch_shapes=[
            pltpu.VMEM((tiles, 128), jnp.float32),
            pltpu.VMEM((9, tiles, CELLS), jnp.float32),
            pltpu.VMEM((2 * tiles, CELLS), jnp.float32),
            pltpu.SemaphoreType.DMA((2,)),
        ],
        compiler_params=pltpu.CompilerParams(vmem_limit_bytes=VMEM_GRANT),
        name="solve",
    )(scores.reshape(tiles, 128), coefs)


def body(patches, windows, candidates, live, edges, stiffness):
    scores, coefs = montage_call(
        patches[0, 0], windows[0, 0], candidates[0, 0], live.transpose(1, 2, 0), edges[0],
        stiffness,
    )
    matches, mesh_shift = solve_call(scores, coefs)
    return (matches.transpose(1, 0, 2)[None, None], mesh_shift[None, None])


def solution(mesh):
    return jax.shard_map(
        body,
        mesh=mesh,
        in_specs=(
            P("row", "col", None, None, None, None),
            P("row", "col", None, None, None),
            P("row", "col", None, None, None),
            P(),
            P("row", None, "col"),
            P("row", "col"),
        ),
        out_specs=(P("row", "col", None, None, None), P("row", "col", None, None)),
        check_vma=False,
    )
```

```python
import functools

import jax
import jax.numpy as jnp
from jax import lax
from jax.experimental import pallas as pl
from jax.experimental.pallas import tpu as pltpu
from jax.sharding import PartitionSpec as P

REACH = 32
WIN = 192
NS = 8
P_SIZE = 16
GV = 16
CELLS = GV * GV
ITERS = 3
GAPS = (1, GV, GV + 1, GV - 1)
CHUNK = 2
PARTS = P_SIZE // CHUNK
PIECES = 1
AHEAD = 4
ROWS_AT = 3
VMEM_GRANT = 56 * 1024 * 1024

LAMBDA_REG = 0.05
EPSILON = 1e-05
PRECISE = lax.Precision.HIGHEST
MESH = pl.DeviceIdType.MESH
HALF = P_SIZE // 2


def lane_of(seam, slot):
    west = jnp.where(slot < HALF, slot * GV, (slot - HALF) * GV + 3)
    north = jnp.where(slot < HALF, slot + 8, slot + 16)
    return jnp.where(seam == 0, west, north)


def turn(values, amount, axis=1):
    return pltpu.roll(values, amount % values.shape[axis], axis)


def rounds_of(count):
    return (count - 1).bit_length()


def partners(me, count, step):
    hop = 1 << step
    if count & (count - 1):
        return lax.rem(me + hop, count), lax.rem(me + count - hop, count)
    other = me + hop - 2 * hop * lax.rem(me // hop, 2)
    return other, other


def montage_kernel(
    sizes, patches, windows, cands, live, edges, stiffness, scores, coefs_out,
    held, frames, flat, plane, red, acc, cand_rows, cand_smem, live_smem, edge_rows, stiff_row,
    springs, coefs, own_row, moves,
    patch_send, patch_recv, cand_send, cand_recv, frame_sem, small_sem,
    col_send, col_recv, row_send, row_recv, score_send, score_recv,
    round_sem,
):
    rows, cols = sizes
    tiles = rows * cols
    me_row = lax.axis_index("row")
    me_col = lax.axis_index("col")
    me = me_row * cols + me_col
    gives = (me_col < cols - 1, me_row < rows - 1)
    takes = (me_col > 0, me_row > 0)
    ahead = ((me_row, me_col + 1), (me_row + 1, me_col))
    pitch = windows.shape[-1] // 128 + 1
    patch_size = patches.shape[-1]
    half = patch_size // 2
    pixel_count = float(patch_size * patch_size)

    def wrap(value, count):
        return jnp.where(value >= count, value - count, value)

    def each_peer(act):
        for step in range(1, cols):
            act(me_row, wrap(me_col + step, cols))

        def one_row(step, carry):
            for col_step in range(cols):
                act(wrap(me_row + step, rows), wrap(me_col + col_step, cols))
            return carry

        lax.fori_loop(1, rows, one_row, 0)

    lanes_each = windows.shape[-1] // PIECES

    def frame_copy(seam, piece):
        span = pl.ds(piece * lanes_each, lanes_each)
        return pltpu.make_async_copy(
            windows.at[seam, :, span], frames.at[seam, :, span], frame_sem.at[seam, piece]
        )

    smalls = [
        pltpu.make_async_copy(edges, edge_rows, small_sem.at[0]),
        pltpu.make_async_copy(stiffness, stiff_row, small_sem.at[1]),
        pltpu.make_async_copy(live, live_smem, small_sem.at[2]),
    ]

    barrier = pltpu.get_barrier_semaphore()
    near = [
        (gives[0], (me_row, me_col + 1)), (gives[1], (me_row + 1, me_col)),
        (takes[0], (me_row, me_col - 1)), (takes[1], (me_row - 1, me_col)),
    ]
    expected = jnp.int32(0)
    for exists, device in near:
        @pl.when(exists)
        def _():
            pl.semaphore_signal(barrier, inc=1, device_id=device, device_id_type=MESH)
        expected = expected + exists.astype(jnp.int32)
    stages = [("col", step) for step in range(rounds_of(cols))]
    stages += [("row", step) for step in range(rounds_of(rows))]

    def stage_partners(stage):
        axis, step = stages[stage]
        if axis == "col":
            return [(me_row, col) for col in partners(me_col, cols, step)]
        return [(row, me_col) for row in partners(me_row, rows, step)]

    for stage, (axis, step) in enumerate(stages):
        count = cols if axis == "col" else rows
        pair = stage_partners(stage)
        if count & (count - 1) == 0:
            pair = pair[:1] if step else []
        for device in pair:
            pl.semaphore_signal(barrier, inc=1, device_id=device, device_id_type=MESH)
        expected = expected + len(pair)
    for copy in smalls:
        copy.start()
    for seam in (1, 0):
        for piece in range(PIECES):
            frame_copy(seam, piece).start()
    pl.semaphore_wait(barrier, expected)

    def cand_copy(seam):
        return pltpu.make_async_remote_copy(
            src_ref=cands.at[seam], dst_ref=cand_rows.at[seam],
            send_sem=cand_send.at[seam], recv_sem=cand_recv.at[seam],
            device_id=ahead[seam], device_id_type=MESH,
        )

    def patch_copy(seam, part):
        span = pl.ds(part * CHUNK, CHUNK)
        return pltpu.make_async_remote_copy(
            src_ref=patches.at[seam, span], dst_ref=held.at[seam, span],
            send_sem=patch_send.at[seam, part], recv_sem=patch_recv.at[seam, part],
            device_id=ahead[seam], device_id_type=MESH,
        )

    for part in range(AHEAD):
        for seam in range(2):
            @pl.when(gives[seam])
            def _():
                patch_copy(seam, part).start()
                if part == 0:
                    cand_copy(seam).start()

    def say(stage):
        pl.semaphore_signal(
            round_sem.at[stage], inc=1, device_id=stage_partners(stage)[0], device_id_type=MESH
        )

    def hear(stage):
        pl.semaphore_wait(round_sem.at[stage], 1)
        if stage + 1 < len(stages):
            say(stage + 1)

    col_stages = rounds_of(cols)
    say(0)

    smalls[0].wait()
    smalls[1].wait()
    first, second = edge_rows[0:1, :], edge_rows[1:2, :]
    lower = jnp.minimum(first, second)
    gap = jnp.abs(first - second)
    kind = lax.broadcasted_iota(jnp.int32, (8, 1), 0)
    wanted = jnp.where(
        kind == 0, GAPS[0], jnp.where(kind == 1, GAPS[1], jnp.where(kind == 2, GAPS[2], GAPS[3]))
    )
    wanted = jnp.where(kind < 4, wanted, -1)
    coarse = stiff_row[...].astype(jnp.bfloat16).astype(jnp.float32)
    rest = stiff_row[...] - coarse
    middle = rest.astype(jnp.bfloat16).astype(jnp.float32)
    strength = jnp.concatenate(
        [jnp.where(gap == wanted, level, 0.0) for level in (coarse, middle, rest - middle)], axis=0
    ).astype(jnp.bfloat16)
    vertex = lax.broadcasted_iota(jnp.int32, (CELLS, lower.shape[1]), 0)
    starts = jnp.where(vertex == lower, 1.0, 0.0).astype(jnp.bfloat16)
    levels = lax.dot_general(
        strength, starts, (((1,), (1,)), ((), ())), preferred_element_type=jnp.float32
    )
    dense = levels[:8] + levels[8:16] + levels[16:]
    mine = pl.ds(pl.multiple_of(me * 8, 8), 8)
    springs[mine, :] = jnp.concatenate([dense[:4, :128], dense[:4, 128:]], axis=0)
    hear(0)

    def send_springs():
        for step in range(1, cols):
            pltpu.make_async_remote_copy(
                src_ref=springs.at[mine], dst_ref=springs.at[mine],
                send_sem=col_send, recv_sem=col_recv,
                device_id=(me_row, wrap(me_col + step, cols)), device_id_type=MESH,
            ).start()

    def cols_all():
        block = springs.at[pl.ds(0, (cols - 1) * 8)]
        return pltpu.make_async_remote_copy(
            src_ref=block, dst_ref=block, send_sem=col_send, recv_sem=col_recv,
            device_id=(me_row, wrap(me_col + 1, cols)), device_id_type=MESH,
        )

    def rows_all():
        block = springs.at[pl.ds(0, (rows - 1) * cols * 8)]
        return pltpu.make_async_remote_copy(
            src_ref=block, dst_ref=block, send_sem=row_send, recv_sem=row_recv,
            device_id=(wrap(me_row + 1, rows), me_col), device_id_type=MESH,
        )

    for seam in (1, 0):
        for piece in range(PIECES):
            frame_copy(seam, piece).wait()

        @pl.when(takes[seam])
        def _():
            def spread_chunk(chunk, carry):
                start = pl.multiple_of(chunk * 128, 128)
                values = frames[seam, :, pl.ds(start, 128)].astype(jnp.float32)
                flat[pl.ds(seam * P_SIZE * pitch + chunk, P_SIZE, stride=pitch), :] = values
                return carry

            lax.fori_loop(0, pitch - 1, spread_chunk, 0, unroll=16)

        if seam == 1:
            for stage in range(1, col_stages):
                hear(stage)
            send_springs()

    for seam in range(2):
        @pl.when(jnp.logical_not(takes[seam]))
        def _():
            cand_rows[seam] = jnp.zeros(cand_rows.shape[1:], jnp.int32)

        @pl.when(takes[seam])
        def _():
            cand_copy(seam).wait_recv()

    to_smem = pltpu.make_async_copy(cand_rows, cand_smem, small_sem.at[3])
    to_smem.start()
    acc[...] = jnp.zeros_like(acc)
    index = lax.broadcasted_iota(jnp.int32, (8, 128), 1)
    member = lax.broadcasted_iota(jnp.int32, (8, 128), 0)
    pick = index % NS == member
    listed = [
        jnp.concatenate(
            [jnp.where(pick, cand_rows[seam, axis : axis + 1, :].astype(jnp.float32), 0.0)
             for seam in range(2)], axis=1,
        )
        for axis in range(2)
    ]
    listed = jnp.concatenate(listed, axis=0).astype(jnp.bfloat16)
    source = lax.broadcasted_iota(jnp.int32, (2 * P_SIZE * NS, 128), 0)
    target = lax.broadcasted_iota(jnp.int32, (2 * P_SIZE * NS, 128), 1)
    place = lane_of(
        jnp.where(source < P_SIZE * NS, 0, 1), (source % (P_SIZE * NS)) // NS
    )
    moves[...] = jnp.dot(
        listed, jnp.where(target == place, 1.0, 0.0).astype(jnp.bfloat16),
        preferred_element_type=jnp.float32,
    )
    lane8 = lax.broadcasted_iota(jnp.int32, (8, 128), 1)
    lane = lax.broadcasted_iota(jnp.int32, (half, 128), 1)
    to_smem.wait()
    smalls[2].wait()

    def fold(values):
        return jnp.sum(values.reshape(half // 8, 8, 128), axis=0)

    def one_slot(seam, slot):
        plane[...] = held[seam, slot].astype(jnp.float32)
        parts = [plane[pl.ds(parity, half, stride=2), :] for parity in range(2)]
        own_sum = fold(parts[0] + parts[1])
        own_square = fold(parts[0] * parts[0] + parts[1] * parts[1])
        base = seam * P_SIZE * pitch + slot * pitch
        for cand in range(NS):
            row = REACH + cand_smem[seam, 0, slot * NS + cand]
            col = REACH + cand_smem[seam, 1, slot * NS + cand]
            crop_sum = crop_square = cross_sum = 0.0
            for parity in range(2):
                place = (row + parity) * WIN + col
                chunk = base + lax.shift_right_logical(place, 7)
                offset = lax.bitwise_and(place, 127)
                low = flat[pl.ds(chunk, half, stride=3), :]
                high = flat[pl.ds(chunk + 1, half, stride=3), :]
                crop = jnp.where(lane >= offset, low, high)
                patch = pltpu.roll(plane[pl.ds(parity, half, stride=2), :], offset, 1)
                crop_sum = crop_sum + fold(crop)
                crop_square = crop_square + fold(crop * crop)
                cross_sum = cross_sum + fold(crop * patch)
            for which, value in enumerate((crop_sum, crop_square, cross_sum)):
                red[which, cand * 8 : cand * 8 + 8, :] = value
        here = lane8 == lane_of(seam, slot)
        for which in range(5):
            if which < 3:
                value = red[which, pl.ds(0, NS, stride=8), :]
                for part in range(1, 8):
                    value = value + red[which, pl.ds(part, NS, stride=8), :]
            else:
                value = (own_sum, own_square)[which - 3]
            acc[which] = jnp.where(here, jnp.sum(value, axis=1, keepdims=True), acc[which])

    coefs_copy = pltpu.make_async_copy(coefs, coefs_out, small_sem.at[4])

    def spring_class(which):
        return jnp.concatenate(
            [springs[pl.ds(part * 4 + which, tiles, stride=8), :] for part in range(2)], axis=1
        )

    def one_part(part, carry):
        for seam in range(2):
            @pl.when(gives[seam])
            def _():
                patch_copy(seam, part).wait_send()

            @pl.when(gives[seam] & (part + AHEAD < PARTS))
            def _():
                patch_copy(seam, part + AHEAD).start()

        for stage in range(col_stages, len(stages)):
            @pl.when(part == max(ROWS_AT - (len(stages) - 1 - stage), 0))
            def _():
                hear(stage)

        @pl.when(part == ROWS_AT)
        def _():
            cols_all().wait_recv()
            band = pl.ds(pl.multiple_of(me_row * cols * 8, 8), cols * 8)

            def send_band(step, inner):
                pltpu.make_async_remote_copy(
                    src_ref=springs.at[band], dst_ref=springs.at[band],
                    send_sem=row_send, recv_sem=row_recv,
                    device_id=(wrap(me_row + step, rows), me_col), device_id_type=MESH,
                ).start()
                return inner

            lax.fori_loop(1, rows, send_band, 0)

        for seam in (1, 0):
            @pl.when(takes[seam])
            def _():
                patch_copy(seam, part).wait_recv()

                def slot_step(step, inner):
                    one_slot(seam, part * CHUNK + step)
                    return inner

                lax.fori_loop(0, CHUNK, slot_step, 0)
        return carry

    lax.fori_loop(0, PARTS, one_part, 0)

    crop_mean, crop_square, cross_mean = [acc[n] / pixel_count for n in range(3)]
    patch_mean, patch_square = [
        jnp.sum(acc[n], axis=0, keepdims=True) / pixel_count for n in (3, 4)
    ]
    patch_var = patch_square - patch_mean * patch_mean
    crop_var = crop_square - crop_mean * crop_mean
    cross = cross_mean - patch_mean * crop_mean
    correl = cross / jnp.sqrt((patch_var + EPSILON) * (crop_var + EPSILON))
    weight = (1.5 + correl) * (1.5 + correl)
    weight_sum = jnp.sum(weight, axis=0, keepdims=True)
    along_y = jnp.sum(weight * moves[:8, :], axis=0, keepdims=True) / (REACH * weight_sum)
    along_x = jnp.sum(weight * moves[8:, :], axis=0, keepdims=True) / (REACH * weight_sum)
    spot = lax.broadcasted_iota(jnp.int32, (1, 128), 1)
    group, within = spot // GV, spot % GV
    counts = (
        jnp.where(takes[0], live_smem[jnp.maximum(me_col - 1, 0), 0, me_row], 0),
        jnp.where(takes[1], live_smem[me_col, 1, jnp.maximum(me_row - 1, 0)], 0),
    )
    western = ((within == 0) & (group < counts[0])) | ((within == 3) & (group + HALF < counts[0]))
    northern = (within >= 8) & (
        ((group == 0) & (spot - 8 < counts[1])) | ((group == 1) & (spot - 16 < counts[1]))
    )
    confidence = jnp.where(western | northern, weight_sum / NS, 0.0)
    row = confidence
    for offset, values in ((1, along_y), (2, along_x)):
        row = row + turn(jnp.where(western, values, 0.0), offset)
    for offset, values in ((32, along_y), (64, along_x)):
        row = row + turn(jnp.where(northern, values, 0.0), offset)
    own_row[...] = row
    own_copy = pltpu.make_async_copy(own_row, scores.at[me], small_sem.at[5])
    own_copy.start()

    each_peer(
        lambda there_row, there_col: pltpu.make_async_remote_copy(
            src_ref=own_row, dst_ref=scores.at[me],
            send_sem=score_send, recv_sem=score_recv,
            device_id=(there_row, there_col), device_id_type=MESH,
        ).start()
    )
    others = scores.at[pl.ds(0, tiles - 1)]
    scores_all = pltpu.make_async_remote_copy(
        src_ref=others, dst_ref=others, send_sem=score_send, recv_sem=score_recv,
        device_id=(me_row, wrap(me_col + 1, cols)), device_id_type=MESH,
    )
    rows_all().wait_recv()
    right, down, diag, anti = [spring_class(which) for which in range(4)]
    coefs[0] = right
    coefs[1] = turn(diag, GV)
    coefs[2] = turn(anti, -1)
    coefs[3] = turn(right, 1)
    coefs[4] = turn(diag, 1)
    coefs[5] = turn(anti, GV)
    coefs[6] = down
    coefs[7] = turn(down, GV)
    coefs[8] = (
        LAMBDA_REG + right + coefs[3] + down + coefs[7]
        + diag + turn(diag, GV + 1) + anti + turn(anti, GV - 1)
    )
    coefs_copy.start()

    scores_all.wait_recv()

    own_copy.wait()
    coefs_copy.wait()
    scores_all.wait_send()
    cols_all().wait_send()
    rows_all().wait_send()
    for seam in range(2):
        @pl.when(gives[seam])
        def _():
            cand_copy(seam).wait_send()


def solve_kernel(
    sizes, scores_in, coefs_in, matches_out, shift_out, scores, coefs, field, matches, shift, sem
):
    rows, cols = sizes
    tiles = rows * cols
    me_row = lax.axis_index("row")
    me_col = lax.axis_index("col")
    me = me_row * cols + me_col
    gives = (me_col < cols - 1, me_row < rows - 1)
    fetches = [
        pltpu.make_async_copy(scores_in, scores, sem.at[0]),
        pltpu.make_async_copy(coefs_in, coefs, sem.at[1]),
    ]
    for copy in fetches:
        copy.start()
    fetches[0].wait()

    source = lax.broadcasted_iota(jnp.int32, (128, 128), 0)
    target = lax.broadcasted_iota(jnp.int32, (128, 128), 1)
    slot, quantity = target % P_SIZE, target // P_SIZE
    quantity = jnp.where(quantity == 2, 0, quantity + 1)
    for seam in range(2):
        near = ((me_row, jnp.minimum(me_col + 1, cols - 1)),
                (jnp.minimum(me_row + 1, rows - 1), me_col))[seam]
        values = jnp.where(gives[seam], scores[pl.ds(near[0] * cols + near[1], 1), :], 0.0)
        spread = (1, 32)[seam]
        chosen = source == lane_of(seam, slot) + quantity * spread
        chosen = jnp.where(chosen & (target < 3 * P_SIZE), 1.0, 0.0)
        packed = jnp.dot(
            jnp.concatenate([values, jnp.zeros((7, 128), jnp.float32)], axis=0), chosen,
            precision=PRECISE, preferred_element_type=jnp.float32,
        )
        for which in range(3):
            matches[which, seam : seam + 1, :] = packed[
                0:1, which * P_SIZE : (which + 1) * P_SIZE
            ]
    matches_copy = pltpu.make_async_copy(matches, matches_out, sem.at[2])
    matches_copy.start()

    table = scores[...]
    spot = lax.broadcasted_iota(jnp.int32, (tiles, 128), 1)
    west_lane = spot % GV == 0

    def westward(which):
        return jnp.concatenate(
            [jnp.where(west_lane, turn(table, -(which + 3 * part)), 0.0) for part in range(2)],
            axis=1,
        )

    def northward(which):
        low = turn(table, -(8 + 32 * which))
        high = turn(table, -(16 + 32 * which))
        near = jnp.where(spot < 8, low, jnp.where(spot < 16, high, 0.0))
        return jnp.concatenate([near, jnp.zeros_like(near)], axis=1)

    west, north = westward(0), northward(0)

    def eastern(values):
        return turn(turn(values, GV - 1), -1, 0)

    def southern(values):
        return turn(turn(values, -GV), -cols, 0)

    fetches[1].wait()
    center = coefs[8] + west + north + eastern(west) + southern(north)
    forces = []
    for axis in range(2):
        pull_west, pull_north = west * westward(axis + 1), north * northward(axis + 1)
        forces.append(eastern(pull_west) + southern(pull_north) - pull_west - pull_north)

    def both(values):
        return jnp.concatenate([values, values], axis=0)

    center = both(center)
    forcing = jnp.concatenate(forces, axis=0)
    seam_west = both(turn(west, -1))
    seam_east = both(turn(west, GV))
    seam_south = both(turn(north, -GV))
    seam_north = both(north)

    def operate(vector):
        below, above = turn(vector, -GV), turn(vector, GV)
        onward = both(coefs[0]) * vector + both(coefs[1]) * above + both(coefs[2]) * below
        onward = onward + seam_west * turn(below, 1, 0)
        backward = both(coefs[3]) * vector + both(coefs[4]) * below + both(coefs[5]) * above
        backward = backward + turn(seam_east * above, -1, 0)
        straight = both(coefs[6]) * below + both(coefs[7]) * above
        straight = straight + turn(seam_south * below, -cols, 0)
        straight = straight + seam_north * turn(above, cols, 0)
        return center * vector - straight - turn(onward, 1) - turn(backward, -1)

    def total(values):
        values = values.reshape(2 * tiles // 8, 8, CELLS)
        values = jnp.sum(values, axis=0)
        values = values[:, :128] + values[:, 128:]
        return jnp.sum(jnp.sum(values, axis=0, keepdims=True), axis=1, keepdims=True)

    residual = forcing
    direction = forcing
    answer = jnp.zeros_like(forcing)
    norm_now = total(residual * residual)
    for iteration in range(ITERS):
        image = operate(direction)
        step_length = norm_now / total(direction * image)
        answer = answer + step_length * direction
        if iteration + 1 < ITERS:
            residual = residual - step_length * image
            norm_next = total(residual * residual)
            direction = residual + (norm_next / norm_now) * direction
            norm_now = norm_next
    field[...] = answer
    shift[...] = jnp.concatenate(
        [field[pl.ds(me, 1), :], field[pl.ds(tiles + me, 1), :]], axis=0
    )
    shift_copy = pltpu.make_async_copy(shift, shift_out, sem.at[3])
    shift_copy.start()
    matches_copy.wait()
    shift_copy.wait()


def montage_call(patches, windows, cands, live, edges, stiffness):
    rows = lax.axis_size("row")
    cols = lax.axis_size("col")
    tiles = rows * cols
    patch_size = patches.shape[-1]
    pitch = windows.shape[-1] // 128 + 1
    anywhere = pl.BlockSpec(memory_space=pl.ANY)
    dma = pltpu.SemaphoreType.DMA
    f32 = jnp.float32
    return pl.pallas_call(
        functools.partial(montage_kernel, (rows, cols)),
        out_shape=(
            jax.ShapeDtypeStruct((tiles, 1, 128), f32),
            jax.ShapeDtypeStruct((9, tiles, CELLS), f32),
        ),
        in_specs=[anywhere] * 6,
        out_specs=(anywhere, anywhere),
        scratch_shapes=[
            pltpu.VMEM(patches.shape, patches.dtype),
            pltpu.VMEM(windows.shape, windows.dtype),
            pltpu.VMEM((2 * P_SIZE * pitch, 128), f32),
            pltpu.VMEM((patch_size, patch_size), f32),
            pltpu.VMEM((3, NS * 8, 128), f32),
            pltpu.VMEM((5, 8, 128), f32),
            pltpu.VMEM(cands.shape, cands.dtype),
            pltpu.SMEM(cands.shape, cands.dtype),
            pltpu.SMEM(live.shape, live.dtype),
            pltpu.VMEM(edges.shape, edges.dtype),
            pltpu.VMEM(stiffness.shape, stiffness.dtype),
            pltpu.VMEM((tiles * 8, 128), f32),
            pltpu.VMEM((9, tiles, CELLS), f32),
            pltpu.VMEM((1, 128), f32),
            pltpu.VMEM((2 * NS, 128), f32),
            dma((2, PARTS)),
            dma((2, PARTS)),
            dma((2,)),
            dma((2,)),
            dma((2, PIECES)),
            dma((6,)),
            dma, dma, dma, dma, dma, dma,
            pltpu.SemaphoreType.REGULAR((rounds_of(rows) + rounds_of(cols),)),
        ],
        compiler_params=pltpu.CompilerParams(
            collective_id=0, has_side_effects=True, vmem_limit_bytes=VMEM_GRANT
        ),
        name="montage",
    )(patches, windows, cands, live, edges, stiffness)


def solve_call(scores, coefs):
    rows = lax.axis_size("row")
    cols = lax.axis_size("col")
    tiles = rows * cols
    anywhere = pl.BlockSpec(memory_space=pl.ANY)
    return pl.pallas_call(
        functools.partial(solve_kernel, (rows, cols)),
        out_shape=(
            jax.ShapeDtypeStruct((3, 2, P_SIZE), jnp.float32),
            jax.ShapeDtypeStruct((2, CELLS), jnp.float32),
        ),
        in_specs=[anywhere, anywhere],
        out_specs=(anywhere, anywhere),
        scratch_shapes=[
            pltpu.VMEM((tiles, 128), jnp.float32),
            pltpu.VMEM((9, tiles, CELLS), jnp.float32),
            pltpu.VMEM((2 * tiles, CELLS), jnp.float32),
            pltpu.VMEM((3, 2, P_SIZE), jnp.float32),
            pltpu.VMEM((2, CELLS), jnp.float32),
            pltpu.SemaphoreType.DMA((4,)),
        ],
        compiler_params=pltpu.CompilerParams(vmem_limit_bytes=VMEM_GRANT),
        name="solve",
    )(scores.reshape(tiles, 128), coefs)


def body(patches, windows, candidates, live, edges, stiffness):
    scores, coefs = montage_call(
        patches[0, 0], windows[0, 0], candidates[0, 0], live.transpose(1, 2, 0), edges[0],
        stiffness,
    )
    matches, mesh_shift = solve_call(scores, coefs)
    return (matches.transpose(1, 0, 2)[None, None], mesh_shift[None, None])


def solution(mesh):
    return jax.shard_map(
        body,
        mesh=mesh,
        in_specs=(
            P("row", "col", None, None, None, None),
            P("row", "col", None, None, None),
            P("row", "col", None, None, None),
            P(),
            P("row", None, "col"),
            P("row", "col"),
        ),
        out_specs=(P("row", "col", None, None, None), P("row", "col", None, None)),
        check_vma=False,
    )
```

```python
import functools

import jax
import jax.numpy as jnp
from jax import lax
from jax.experimental import pallas as pl
from jax.experimental.pallas import tpu as pltpu
from jax.sharding import PartitionSpec as P

REACH = 32
WIN = 192
NS = 8
P_SIZE = 16
GV = 16
CELLS = GV * GV
ITERS = 3
GAPS = (1, GV, GV + 1, GV - 1)
CHUNK = 2
PARTS = P_SIZE // CHUNK
PIECES = 1
AHEAD = 4
ROWS_AT = 3
VMEM_GRANT = 56 * 1024 * 1024

LAMBDA_REG = 0.05
EPSILON = 1e-05
PRECISE = lax.Precision.HIGHEST
MESH = pl.DeviceIdType.MESH
HALF = P_SIZE // 2


def lane_of(seam, slot):
    west = jnp.where(slot < HALF, slot * GV, (slot - HALF) * GV + 3)
    north = jnp.where(slot < HALF, slot + 8, slot + 16)
    return jnp.where(seam == 0, west, north)


def turn(values, amount, axis=1):
    return pltpu.roll(values, amount % values.shape[axis], axis)


def rounds_of(count):
    return (count - 1).bit_length()


def partners(me, count, step):
    hop = 1 << step
    if count & (count - 1):
        return lax.rem(me + hop, count), lax.rem(me + count - hop, count)
    other = me + hop - 2 * hop * lax.rem(me // hop, 2)
    return other, other


def montage_kernel(
    sizes, patches, windows, cands, live, edges, stiffness, scores, coefs_out,
    held, frames, flat, plane, red, acc, cand_rows, cand_smem, live_smem, edge_rows, stiff_row,
    springs, coefs, own_row, moves,
    patch_send, patch_recv, cand_send, cand_recv, frame_sem, small_sem,
    col_send, col_recv, row_send, row_recv, score_send, score_recv,
    round_sem,
):
    rows, cols = sizes
    tiles = rows * cols
    me_row = lax.axis_index("row")
    me_col = lax.axis_index("col")
    me = me_row * cols + me_col
    gives = (me_col < cols - 1, me_row < rows - 1)
    takes = (me_col > 0, me_row > 0)
    ahead = ((me_row, me_col + 1), (me_row + 1, me_col))
    pitch = windows.shape[-1] // 128 + 1
    patch_size = patches.shape[-1]
    half = patch_size // 2
    pixel_count = float(patch_size * patch_size)

    def wrap(value, count):
        return jnp.where(value >= count, value - count, value)

    def each_peer(act):
        for step in range(1, cols):
            act(me_row, wrap(me_col + step, cols))

        def one_row(step, carry):
            for col_step in range(cols):
                act(wrap(me_row + step, rows), wrap(me_col + col_step, cols))
            return carry

        lax.fori_loop(1, rows, one_row, 0)

    lanes_each = windows.shape[-1] // PIECES

    def frame_copy(seam, piece):
        span = pl.ds(piece * lanes_each, lanes_each)
        return pltpu.make_async_copy(
            windows.at[seam, :, span], frames.at[seam, :, span], frame_sem.at[seam, piece]
        )

    smalls = [
        pltpu.make_async_copy(edges, edge_rows, small_sem.at[0]),
        pltpu.make_async_copy(stiffness, stiff_row, small_sem.at[1]),
        pltpu.make_async_copy(live, live_smem, small_sem.at[2]),
    ]

    barrier = pltpu.get_barrier_semaphore()
    near = [
        (gives[0], (me_row, me_col + 1)), (gives[1], (me_row + 1, me_col)),
        (takes[0], (me_row, me_col - 1)), (takes[1], (me_row - 1, me_col)),
    ]
    expected = jnp.int32(0)
    for exists, device in near:
        @pl.when(exists)
        def _():
            pl.semaphore_signal(barrier, inc=1, device_id=device, device_id_type=MESH)
        expected = expected + exists.astype(jnp.int32)
    stages = [("col", step) for step in range(rounds_of(cols))]
    stages += [("row", step) for step in range(rounds_of(rows))]

    def stage_partners(stage):
        axis, step = stages[stage]
        if axis == "col":
            return [(me_row, col) for col in partners(me_col, cols, step)]
        return [(row, me_col) for row in partners(me_row, rows, step)]

    for stage, (axis, step) in enumerate(stages):
        count = cols if axis == "col" else rows
        pair = stage_partners(stage)
        if count & (count - 1) == 0:
            pair = pair[:1] if step else []
        for device in pair:
            pl.semaphore_signal(barrier, inc=1, device_id=device, device_id_type=MESH)
        expected = expected + len(pair)
    for copy in smalls:
        copy.start()
    for seam in (1, 0):
        @pl.when(takes[seam])
        def _():
            for piece in range(PIECES):
                frame_copy(seam, piece).start()
    pl.semaphore_wait(barrier, expected)

    def cand_copy(seam):
        return pltpu.make_async_remote_copy(
            src_ref=cands.at[seam], dst_ref=cand_rows.at[seam],
            send_sem=cand_send.at[seam], recv_sem=cand_recv.at[seam],
            device_id=ahead[seam], device_id_type=MESH,
        )

    def patch_copy(seam, part):
        span = pl.ds(part * CHUNK, CHUNK)
        return pltpu.make_async_remote_copy(
            src_ref=patches.at[seam, span], dst_ref=held.at[seam, span],
            send_sem=patch_send.at[seam, part], recv_sem=patch_recv.at[seam, part],
            device_id=ahead[seam], device_id_type=MESH,
        )

    for part in range(AHEAD):
        for seam in range(2):
            @pl.when(gives[seam])
            def _():
                patch_copy(seam, part).start()
                if part == 0:
                    cand_copy(seam).start()

    def say(stage):
        pl.semaphore_signal(
            round_sem.at[stage], inc=1, device_id=stage_partners(stage)[0], device_id_type=MESH
        )

    def hear(stage):
        pl.semaphore_wait(round_sem.at[stage], 1)
        if stage + 1 < len(stages):
            say(stage + 1)

    col_stages = rounds_of(cols)
    say(0)

    smalls[0].wait()
    smalls[1].wait()
    first, second = edge_rows[0:1, :], edge_rows[1:2, :]
    lower = jnp.minimum(first, second)
    gap = jnp.abs(first - second)
    kind = lax.broadcasted_iota(jnp.int32, (8, 1), 0)
    wanted = jnp.where(
        kind == 0, GAPS[0], jnp.where(kind == 1, GAPS[1], jnp.where(kind == 2, GAPS[2], GAPS[3]))
    )
    wanted = jnp.where(kind < 4, wanted, -1)
    coarse = stiff_row[...].astype(jnp.bfloat16).astype(jnp.float32)
    rest = stiff_row[...] - coarse
    middle = rest.astype(jnp.bfloat16).astype(jnp.float32)
    strength = jnp.concatenate(
        [jnp.where(gap == wanted, level, 0.0) for level in (coarse, middle, rest - middle)], axis=0
    ).astype(jnp.bfloat16)
    vertex = lax.broadcasted_iota(jnp.int32, (CELLS, lower.shape[1]), 0)
    starts = jnp.where(vertex == lower, 1.0, 0.0).astype(jnp.bfloat16)
    levels = lax.dot_general(
        strength, starts, (((1,), (1,)), ((), ())), preferred_element_type=jnp.float32
    )
    dense = levels[:8] + levels[8:16] + levels[16:]
    mine = pl.ds(pl.multiple_of(me * 8, 8), 8)
    springs[mine, :] = jnp.concatenate([dense[:4, :128], dense[:4, 128:]], axis=0)
    hear(0)

    def send_springs():
        for step in range(1, cols):
            pltpu.make_async_remote_copy(
                src_ref=springs.at[mine], dst_ref=springs.at[mine],
                send_sem=col_send, recv_sem=col_recv,
                device_id=(me_row, wrap(me_col + step, cols)), device_id_type=MESH,
            ).start()

    def cols_all():
        block = springs.at[pl.ds(0, (cols - 1) * 8)]
        return pltpu.make_async_remote_copy(
            src_ref=block, dst_ref=block, send_sem=col_send, recv_sem=col_recv,
            device_id=(me_row, wrap(me_col + 1, cols)), device_id_type=MESH,
        )

    def rows_all():
        block = springs.at[pl.ds(0, (rows - 1) * cols * 8)]
        return pltpu.make_async_remote_copy(
            src_ref=block, dst_ref=block, send_sem=row_send, recv_sem=row_recv,
            device_id=(wrap(me_row + 1, rows), me_col), device_id_type=MESH,
        )

    for seam in (1, 0):
        @pl.when(takes[seam])
        def _():
            for piece in range(PIECES):
                frame_copy(seam, piece).wait()

            def spread_chunk(chunk, carry):
                start = pl.multiple_of(chunk * 128, 128)
                values = frames[seam, :, pl.ds(start, 128)].astype(jnp.float32)
                flat[pl.ds(seam * P_SIZE * pitch + chunk, P_SIZE, stride=pitch), :] = values
                return carry

            lax.fori_loop(0, pitch - 1, spread_chunk, 0, unroll=16)

        if seam == 1:
            for stage in range(1, col_stages):
                hear(stage)
            send_springs()

    for seam in range(2):
        @pl.when(jnp.logical_not(takes[seam]))
        def _():
            cand_rows[seam] = jnp.zeros(cand_rows.shape[1:], jnp.int32)

        @pl.when(takes[seam])
        def _():
            cand_copy(seam).wait_recv()

    to_smem = pltpu.make_async_copy(cand_rows, cand_smem, small_sem.at[3])
    to_smem.start()
    acc[...] = jnp.zeros_like(acc)
    index = lax.broadcasted_iota(jnp.int32, (8, 128), 1)
    member = lax.broadcasted_iota(jnp.int32, (8, 128), 0)
    pick = index % NS == member
    listed = [
        jnp.concatenate(
            [jnp.where(pick, cand_rows[seam, axis : axis + 1, :].astype(jnp.float32), 0.0)
             for seam in range(2)], axis=1,
        )
        for axis in range(2)
    ]
    listed = jnp.concatenate(listed, axis=0).astype(jnp.bfloat16)
    source = lax.broadcasted_iota(jnp.int32, (2 * P_SIZE * NS, 128), 0)
    target = lax.broadcasted_iota(jnp.int32, (2 * P_SIZE * NS, 128), 1)
    place = lane_of(
        jnp.where(source < P_SIZE * NS, 0, 1), (source % (P_SIZE * NS)) // NS
    )
    moves[...] = jnp.dot(
        listed, jnp.where(target == place, 1.0, 0.0).astype(jnp.bfloat16),
        preferred_element_type=jnp.float32,
    )
    lane8 = lax.broadcasted_iota(jnp.int32, (8, 128), 1)
    lane = lax.broadcasted_iota(jnp.int32, (half, 128), 1)
    to_smem.wait()
    smalls[2].wait()

    def fold(values):
        return jnp.sum(values.reshape(half // 8, 8, 128), axis=0)

    def one_slot(seam, slot):
        plane[...] = held[seam, slot].astype(jnp.float32)
        parts = [plane[pl.ds(parity, half, stride=2), :] for parity in range(2)]
        own_sum = fold(parts[0] + parts[1])
        own_square = fold(parts[0] * parts[0] + parts[1] * parts[1])
        base = seam * P_SIZE * pitch + slot * pitch
        for cand in range(NS):
            row = REACH + cand_smem[seam, 0, slot * NS + cand]
            col = REACH + cand_smem[seam, 1, slot * NS + cand]
            crop_sum = crop_square = cross_sum = 0.0
            for parity in range(2):
                place = (row + parity) * WIN + col
                chunk = base + lax.shift_right_logical(place, 7)
                offset = lax.bitwise_and(place, 127)
                low = flat[pl.ds(chunk, half, stride=3), :]
                high = flat[pl.ds(chunk + 1, half, stride=3), :]
                crop = jnp.where(lane >= offset, low, high)
                patch = pltpu.roll(plane[pl.ds(parity, half, stride=2), :], offset, 1)
                crop_sum = crop_sum + fold(crop)
                crop_square = crop_square + fold(crop * crop)
                cross_sum = cross_sum + fold(crop * patch)
            for which, value in enumerate((crop_sum, crop_square, cross_sum)):
                red[which, cand * 8 : cand * 8 + 8, :] = value
        here = lane8 == lane_of(seam, slot)
        for which in range(5):
            if which < 3:
                value = red[which, pl.ds(0, NS, stride=8), :]
                for part in range(1, 8):
                    value = value + red[which, pl.ds(part, NS, stride=8), :]
            else:
                value = (own_sum, own_square)[which - 3]
            acc[which] = jnp.where(here, jnp.sum(value, axis=1, keepdims=True), acc[which])

    coefs_copy = pltpu.make_async_copy(coefs, coefs_out, small_sem.at[4])

    def spring_class(which):
        return jnp.concatenate(
            [springs[pl.ds(part * 4 + which, tiles, stride=8), :] for part in range(2)], axis=1
        )

    def one_part(part, carry):
        for seam in range(2):
            @pl.when(gives[seam])
            def _():
                patch_copy(seam, part).wait_send()

            @pl.when(gives[seam] & (part + AHEAD < PARTS))
            def _():
                patch_copy(seam, part + AHEAD).start()

        for stage in range(col_stages, len(stages)):
            @pl.when(part == max(ROWS_AT - (len(stages) - 1 - stage), 0))
            def _():
                hear(stage)

        @pl.when(part == ROWS_AT)
        def _():
            cols_all().wait_recv()
            band = pl.ds(pl.multiple_of(me_row * cols * 8, 8), cols * 8)

            def send_band(step, inner):
                pltpu.make_async_remote_copy(
                    src_ref=springs.at[band], dst_ref=springs.at[band],
                    send_sem=row_send, recv_sem=row_recv,
                    device_id=(wrap(me_row + step, rows), me_col), device_id_type=MESH,
                ).start()
                return inner

            lax.fori_loop(1, rows, send_band, 0)

        for seam in (1, 0):
            @pl.when(takes[seam])
            def _():
                patch_copy(seam, part).wait_recv()

                def slot_step(step, inner):
                    one_slot(seam, part * CHUNK + step)
                    return inner

                lax.fori_loop(0, CHUNK, slot_step, 0)
        return carry

    lax.fori_loop(0, PARTS, one_part, 0)

    crop_mean, crop_square, cross_mean = [acc[n] / pixel_count for n in range(3)]
    patch_mean, patch_square = [
        jnp.sum(acc[n], axis=0, keepdims=True) / pixel_count for n in (3, 4)
    ]
    patch_var = patch_square - patch_mean * patch_mean
    crop_var = crop_square - crop_mean * crop_mean
    cross = cross_mean - patch_mean * crop_mean
    correl = cross / jnp.sqrt((patch_var + EPSILON) * (crop_var + EPSILON))
    weight = (1.5 + correl) * (1.5 + correl)
    weight_sum = jnp.sum(weight, axis=0, keepdims=True)
    along_y = jnp.sum(weight * moves[:8, :], axis=0, keepdims=True) / (REACH * weight_sum)
    along_x = jnp.sum(weight * moves[8:, :], axis=0, keepdims=True) / (REACH * weight_sum)
    spot = lax.broadcasted_iota(jnp.int32, (1, 128), 1)
    group, within = spot // GV, spot % GV
    counts = (
        jnp.where(takes[0], live_smem[jnp.maximum(me_col - 1, 0), 0, me_row], 0),
        jnp.where(takes[1], live_smem[me_col, 1, jnp.maximum(me_row - 1, 0)], 0),
    )
    western = ((within == 0) & (group < counts[0])) | ((within == 3) & (group + HALF < counts[0]))
    northern = (within >= 8) & (
        ((group == 0) & (spot - 8 < counts[1])) | ((group == 1) & (spot - 16 < counts[1]))
    )
    confidence = jnp.where(western | northern, weight_sum / NS, 0.0)
    row = confidence
    for offset, values in ((1, along_y), (2, along_x)):
        row = row + turn(jnp.where(western, values, 0.0), offset)
    for offset, values in ((32, along_y), (64, along_x)):
        row = row + turn(jnp.where(northern, values, 0.0), offset)
    own_row[...] = row
    own_copy = pltpu.make_async_copy(own_row, scores.at[me], small_sem.at[5])
    own_copy.start()

    each_peer(
        lambda there_row, there_col: pltpu.make_async_remote_copy(
            src_ref=own_row, dst_ref=scores.at[me],
            send_sem=score_send, recv_sem=score_recv,
            device_id=(there_row, there_col), device_id_type=MESH,
        ).start()
    )
    others = scores.at[pl.ds(0, tiles - 1)]
    scores_all = pltpu.make_async_remote_copy(
        src_ref=others, dst_ref=others, send_sem=score_send, recv_sem=score_recv,
        device_id=(me_row, wrap(me_col + 1, cols)), device_id_type=MESH,
    )
    rows_all().wait_recv()
    right, down, diag, anti = [spring_class(which) for which in range(4)]
    coefs[0] = right
    coefs[1] = turn(diag, GV)
    coefs[2] = turn(anti, -1)
    coefs[3] = turn(right, 1)
    coefs[4] = turn(diag, 1)
    coefs[5] = turn(anti, GV)
    coefs[6] = down
    coefs[7] = turn(down, GV)
    coefs[8] = (
        LAMBDA_REG + right + coefs[3] + down + coefs[7]
        + diag + turn(diag, GV + 1) + anti + turn(anti, GV - 1)
    )
    coefs_copy.start()

    scores_all.wait_recv()

    own_copy.wait()
    coefs_copy.wait()
    scores_all.wait_send()
    cols_all().wait_send()
    rows_all().wait_send()
    for seam in range(2):
        @pl.when(gives[seam])
        def _():
            cand_copy(seam).wait_send()


def solve_kernel(
    sizes, scores_in, coefs_in, matches_out, shift_out, scores, coefs, field, matches, shift, sem
):
    rows, cols = sizes
    tiles = rows * cols
    me_row = lax.axis_index("row")
    me_col = lax.axis_index("col")
    me = me_row * cols + me_col
    gives = (me_col < cols - 1, me_row < rows - 1)
    fetches = [
        pltpu.make_async_copy(scores_in, scores, sem.at[0]),
        pltpu.make_async_copy(coefs_in, coefs, sem.at[1]),
    ]
    for copy in fetches:
        copy.start()
    fetches[0].wait()

    source = lax.broadcasted_iota(jnp.int32, (128, 128), 0)
    target = lax.broadcasted_iota(jnp.int32, (128, 128), 1)
    slot, quantity = target % P_SIZE, target // P_SIZE
    quantity = jnp.where(quantity == 2, 0, quantity + 1)
    for seam in range(2):
        near = ((me_row, jnp.minimum(me_col + 1, cols - 1)),
                (jnp.minimum(me_row + 1, rows - 1), me_col))[seam]
        values = jnp.where(gives[seam], scores[pl.ds(near[0] * cols + near[1], 1), :], 0.0)
        spread = (1, 32)[seam]
        chosen = source == lane_of(seam, slot) + quantity * spread
        chosen = jnp.where(chosen & (target < 3 * P_SIZE), 1.0, 0.0)
        packed = jnp.dot(
            jnp.concatenate([values, jnp.zeros((7, 128), jnp.float32)], axis=0), chosen,
            precision=PRECISE, preferred_element_type=jnp.float32,
        )
        for which in range(3):
            matches[which, seam : seam + 1, :] = packed[
                0:1, which * P_SIZE : (which + 1) * P_SIZE
            ]
    matches_copy = pltpu.make_async_copy(matches, matches_out, sem.at[2])
    matches_copy.start()

    table = scores[...]
    spot = lax.broadcasted_iota(jnp.int32, (tiles, 128), 1)
    west_lane = spot % GV == 0

    def westward(which):
        return jnp.concatenate(
            [jnp.where(west_lane, turn(table, -(which + 3 * part)), 0.0) for part in range(2)],
            axis=1,
        )

    def northward(which):
        low = turn(table, -(8 + 32 * which))
        high = turn(table, -(16 + 32 * which))
        near = jnp.where(spot < 8, low, jnp.where(spot < 16, high, 0.0))
        return jnp.concatenate([near, jnp.zeros_like(near)], axis=1)

    west, north = westward(0), northward(0)

    def eastern(values):
        return turn(turn(values, GV - 1), -1, 0)

    def southern(values):
        return turn(turn(values, -GV), -cols, 0)

    fetches[1].wait()
    center = coefs[8] + west + north + eastern(west) + southern(north)
    forces = []
    for axis in range(2):
        pull_west, pull_north = west * westward(axis + 1), north * northward(axis + 1)
        forces.append(eastern(pull_west) + southern(pull_north) - pull_west - pull_north)

    def both(values):
        return jnp.concatenate([values, values], axis=0)

    center = both(center)
    forcing = jnp.concatenate(forces, axis=0)
    seam_west = both(turn(west, -1))
    seam_east = both(turn(west, GV))
    seam_south = both(turn(north, -GV))
    seam_north = both(north)

    def operate(vector):
        below, above = turn(vector, -GV), turn(vector, GV)
        onward = both(coefs[0]) * vector + both(coefs[1]) * above + both(coefs[2]) * below
        onward = onward + seam_west * turn(below, 1, 0)
        backward = both(coefs[3]) * vector + both(coefs[4]) * below + both(coefs[5]) * above
        backward = backward + turn(seam_east * above, -1, 0)
        straight = both(coefs[6]) * below + both(coefs[7]) * above
        straight = straight + turn(seam_south * below, -cols, 0)
        straight = straight + seam_north * turn(above, cols, 0)
        return center * vector - straight - turn(onward, 1) - turn(backward, -1)

    def total(values):
        values = values.reshape(2 * tiles // 8, 8, CELLS)
        values = jnp.sum(values, axis=0)
        values = values[:, :128] + values[:, 128:]
        return jnp.sum(jnp.sum(values, axis=0, keepdims=True), axis=1, keepdims=True)

    residual = forcing
    direction = forcing
    answer = jnp.zeros_like(forcing)
    norm_now = total(residual * residual)
    for iteration in range(ITERS):
        image = operate(direction)
        step_length = norm_now / total(direction * image)
        answer = answer + step_length * direction
        if iteration + 1 < ITERS:
            residual = residual - step_length * image
            norm_next = total(residual * residual)
            direction = residual + (norm_next / norm_now) * direction
            norm_now = norm_next
    field[...] = answer
    shift[...] = jnp.concatenate(
        [field[pl.ds(me, 1), :], field[pl.ds(tiles + me, 1), :]], axis=0
    )
    shift_copy = pltpu.make_async_copy(shift, shift_out, sem.at[3])
    shift_copy.start()
    matches_copy.wait()
    shift_copy.wait()


def montage_call(patches, windows, cands, live, edges, stiffness):
    rows = lax.axis_size("row")
    cols = lax.axis_size("col")
    tiles = rows * cols
    patch_size = patches.shape[-1]
    pitch = windows.shape[-1] // 128 + 1
    anywhere = pl.BlockSpec(memory_space=pl.ANY)
    dma = pltpu.SemaphoreType.DMA
    f32 = jnp.float32
    return pl.pallas_call(
        functools.partial(montage_kernel, (rows, cols)),
        out_shape=(
            jax.ShapeDtypeStruct((tiles, 1, 128), f32),
            jax.ShapeDtypeStruct((9, tiles, CELLS), f32),
        ),
        in_specs=[anywhere] * 6,
        out_specs=(anywhere, anywhere),
        scratch_shapes=[
            pltpu.VMEM(patches.shape, patches.dtype),
            pltpu.VMEM(windows.shape, windows.dtype),
            pltpu.VMEM((2 * P_SIZE * pitch, 128), f32),
            pltpu.VMEM((patch_size, patch_size), f32),
            pltpu.VMEM((3, NS * 8, 128), f32),
            pltpu.VMEM((5, 8, 128), f32),
            pltpu.VMEM(cands.shape, cands.dtype),
            pltpu.SMEM(cands.shape, cands.dtype),
            pltpu.SMEM(live.shape, live.dtype),
            pltpu.VMEM(edges.shape, edges.dtype),
            pltpu.VMEM(stiffness.shape, stiffness.dtype),
            pltpu.VMEM((tiles * 8, 128), f32),
            pltpu.VMEM((9, tiles, CELLS), f32),
            pltpu.VMEM((1, 128), f32),
            pltpu.VMEM((2 * NS, 128), f32),
            dma((2, PARTS)),
            dma((2, PARTS)),
            dma((2,)),
            dma((2,)),
            dma((2, PIECES)),
            dma((6,)),
            dma, dma, dma, dma, dma, dma,
            pltpu.SemaphoreType.REGULAR((rounds_of(rows) + rounds_of(cols),)),
        ],
        compiler_params=pltpu.CompilerParams(
            collective_id=0, has_side_effects=True, vmem_limit_bytes=VMEM_GRANT
        ),
        name="montage",
    )(patches, windows, cands, live, edges, stiffness)


def solve_call(scores, coefs):
    rows = lax.axis_size("row")
    cols = lax.axis_size("col")
    tiles = rows * cols
    anywhere = pl.BlockSpec(memory_space=pl.ANY)
    return pl.pallas_call(
        functools.partial(solve_kernel, (rows, cols)),
        out_shape=(
            jax.ShapeDtypeStruct((3, 2, P_SIZE), jnp.float32),
            jax.ShapeDtypeStruct((2, CELLS), jnp.float32),
        ),
        in_specs=[anywhere, anywhere],
        out_specs=(anywhere, anywhere),
        scratch_shapes=[
            pltpu.VMEM((tiles, 128), jnp.float32),
            pltpu.VMEM((9, tiles, CELLS), jnp.float32),
            pltpu.VMEM((2 * tiles, CELLS), jnp.float32),
            pltpu.VMEM((3, 2, P_SIZE), jnp.float32),
            pltpu.VMEM((2, CELLS), jnp.float32),
            pltpu.SemaphoreType.DMA((4,)),
        ],
        compiler_params=pltpu.CompilerParams(vmem_limit_bytes=VMEM_GRANT),
        name="solve",
    )(scores.reshape(tiles, 128), coefs)


def body(patches, windows, candidates, live, edges, stiffness):
    scores, coefs = montage_call(
        patches[0, 0], windows[0, 0], candidates[0, 0], live.transpose(1, 2, 0), edges[0],
        stiffness,
    )
    matches, mesh_shift = solve_call(scores, coefs)
    return (matches.transpose(1, 0, 2)[None, None], mesh_shift[None, None])


def solution(mesh):
    return jax.shard_map(
        body,
        mesh=mesh,
        in_specs=(
            P("row", "col", None, None, None, None),
            P("row", "col", None, None, None),
            P("row", "col", None, None, None),
            P(),
            P("row", None, "col"),
            P("row", "col"),
        ),
        out_specs=(P("row", "col", None, None, None), P("row", "col", None, None)),
        check_vma=False,
    )
```
